128 devices in a mesh: req: 4 (over y), kv: 32 (over x, z, core).
Axes of the slice: x: 4, y: 4, z: 4, core: 2. Of those that a mesh axis runs over, the one named last changes fastest.
Arguments:
- stream: bfloat16 [16384, 2048], P(('req', 'kv')), may hold values from -40 to 40
- projections: bfloat16 [16384, 6144], P(('req', 'kv')), may hold values from -32 to 32
- key_cache: bfloat16 [131072, 2048], P(('req', 'kv')), may hold values from -12 to 12
- value_cache: bfloat16 [131072, 2048], P(('req', 'kv')), may hold values from -6 to 6
- cache_range: int32 [16, 2], replicated, may hold values from 0 to 8192, as said below
- norm_gain: float32 [2048], replicated, may hold values from 0.5 to 1.5
- out_weight: bfloat16 [2048, 2048], P(('req', 'kv')), may hold values from -0.125 to 0.125
- up_weight: bfloat16 [8192, 2048], P(('req', 'kv')), may hold values from -0.125 to 0.125
- down_weight: bfloat16 [8192, 2048], P(('req', 'kv')), may hold values from -0.0625 to 0.0625
Outputs:
- layer_out: bfloat16 [16384, 2048], P(('req', 'kv'))
The draws below stay inside these ranges and needn't reach their ends.
Inputs may be any that keep to these rules, and one draw needn't show every extreme that they name: `cache_range`: row r holds the first and the end of the cached positions that request r attends to: 0 <= first < 2048, first < end <= 8192, and end = 8192 for some request.
All inputs are finite; a program needn't handle non-finite values.
Results may differ from the reference program's by a relative error of at most 0.011.
Values may be sent and summed in bfloat16 or wider, within the bound.
No kernel may reach another device: no remote copies, remote signals or barrier semaphores. Data moves between devices by JAX's collectives and lax.ppermute only.
A program may use at most 192 MiB of HBM per device.

```python
import math
import jax
import jax.numpy as jnp
from jax import lax

H = 8
HD = 256
FF = 8192
D = 2048
NEW = 1024
CACHE = 8192
REQS = 16
TOKENS = 16384


def spread_scale(key, shape):
    return jnp.exp(jax.random.uniform(key, shape, jnp.float32, math.log(0.3), math.log(3.0)))


def draw_stream(key, part):
    key_rows, key_cols, key_base = jax.random.split(key, 3)
    row_scale = spread_scale(key_rows, (TOKENS, 1))
    col_scale = spread_scale(key_cols, (1, D))
    base = jax.random.truncated_normal(key_base, -4.0, 4.0, (TOKENS, D), jnp.float32)
    values = base * row_scale * col_scale
    return values.astype(jnp.bfloat16)


def draw_projections(key, part):
    key_base, key_scale = jax.random.split(key, 2)
    base = jax.random.truncated_normal(key_base, -4.0, 4.0, (TOKENS, 3, H, HD), jnp.float32)
    queries = base[:, 0]
    keys = base[:, 1]
    values = base[:, 2]
    scale = spread_scale(key_scale, (TOKENS, H, 1))
    keys = keys * scale
    joined = jnp.stack([queries, keys, values], 1)
    return joined.reshape(TOKENS, 3 * D).astype(jnp.bfloat16)


def draw_key_cache(key, part):
    key_base, key_scale = jax.random.split(key, 2)
    total = REQS * CACHE
    base = jax.random.truncated_normal(key_base, -4.0, 4.0, (total, H, HD), jnp.float32)
    values = base * spread_scale(key_scale, (total, H, 1))
    return values.reshape(total, D).astype(jnp.bfloat16)


def draw_cache_range(key, part):
    key_low, key_span, key_full = jax.random.split(key, 3)
    lower_end = jax.random.randint(key_low, (REQS,), 0, CACHE // 4, jnp.int32)
    extent = CACHE // 8 + jax.random.randint(key_span, (REQS,), 0, CACHE - CACHE // 4 - CACHE // 8 + 1, jnp.int32)
    chosen = jax.random.randint(key_full, (), 0, REQS, jnp.int32)
    upper_end = jnp.where(jnp.arange(REQS, dtype=jnp.int32) == chosen, CACHE, lower_end + extent)
    return jnp.stack([lower_end, upper_end], 1).astype(jnp.int32)


def shard_levels(own_key, dims, cuts, smallest, high):
    level, own = 1.0, jax.random.fold_in(own_key, 6)
    for dim, blocks in cuts:
        draws = jnp.exp(jax.random.uniform(jax.random.fold_in(own, dim), (blocks,), jnp.float32, smallest / len(cuts), high / len(cuts)))
        level = level * jnp.repeat(draws, dims[dim] // blocks).reshape([-1 if axis == dim else 1 for axis in range(len(dims))])
    return level


def normal_values(stream_key, shape, width, reach, pieces=(), kind=jnp.bfloat16):
    drawn = jax.random.normal(stream_key, shape, jnp.float32) * width
    if len(pieces) > 0:
        drawn = shard_levels(stream_key, shape, pieces, -0.22, 0.18) * drawn
    return jnp.clip(drawn, min=-reach, max=reach).astype(kind)


def setup_inputs(seed: int = 0) -> dict:
    seeds = jax.random.split(jax.random.key(seed), 10)
    stream = draw_stream(jax.random.fold_in(seeds[9], 71), 0)
    projections = draw_projections(jax.random.fold_in(seeds[9], 71), 0)
    key_cache = draw_key_cache(jax.random.fold_in(seeds[9], 71), 0)
    value_cache = normal_values(seeds[3], (REQS * CACHE, D), 1.0, 6.0, ((0, 128),))
    cache_range = draw_cache_range(jax.random.fold_in(seeds[9], 71), 0)
    norm_gain = jnp.clip(1.0 + 0.1 * jax.random.normal(seeds[5], (D,), jnp.float32), 0.5, 1.5)
    out_weight = normal_values(seeds[6], (D, D), D ** -0.5, 0.125, ((0, 128),))
    up_weight = normal_values(seeds[7], (FF, D), D ** -0.5, 0.125, ((0, 128),))
    down_weight = normal_values(seeds[8], (FF, D), FF ** -0.5, 0.0625, ((0, 128),))
    return {"stream": stream, "projections": projections, "key_cache": key_cache, "value_cache": value_cache, "cache_range": cache_range, "norm_gain": norm_gain, "out_weight": out_weight, "up_weight": up_weight, "down_weight": down_weight}


def layer_norm(stream, norm_gain):
    values = stream.astype(jnp.float32)
    centred = values - lax.optimization_barrier(jnp.mean(values, axis=-1, keepdims=True))
    spread = lax.optimization_barrier(jnp.mean(centred * centred, axis=-1, keepdims=True))
    return centred * lax.rsqrt(spread + 1e-05) * norm_gain

def reference(stream, projections, key_cache, value_cache, cache_range, norm_gain, out_weight, up_weight, down_weight):
    score_scale = 1.0 / math.sqrt(HD)

    def one_request(index):
        index = index.astype(jnp.int32)
        rows = lax.dynamic_slice_in_dim(projections, index * NEW, NEW, 0)
        queries = rows[:, :D].astype(jnp.float32).reshape(NEW, H, HD)
        new_keys = rows[:, D:2 * D].astype(jnp.float32).reshape(NEW, H, HD)
        new_values = rows[:, 2 * D:].astype(jnp.float32).reshape(NEW, H, HD)
        cached_keys = lax.dynamic_slice_in_dim(key_cache, index * CACHE, CACHE, 0).astype(jnp.float32).reshape(CACHE, H, HD)
        cached_values = lax.dynamic_slice_in_dim(value_cache, index * CACHE, CACHE, 0).astype(jnp.float32).reshape(CACHE, H, HD)
        key_rows = jnp.concatenate([cached_keys, new_keys], 0)
        value_rows = jnp.concatenate([cached_values, new_values], 0)
        lower_end = cache_range[index, 0]
        upper_end = cache_range[index, 1]
        positions = jnp.arange(CACHE, dtype=jnp.int32)
        cache_visible = (positions >= lower_end) & (positions < upper_end)
        token_pos = jnp.arange(NEW, dtype=jnp.int32)
        new_visible = token_pos[None, :] <= token_pos[:, None]
        visible = jnp.concatenate([jnp.broadcast_to(cache_visible[None, :], (NEW, CACHE)), new_visible], 1)
        scores = jnp.einsum('qhd,khd->hqk', queries, key_rows) * score_scale
        scores = jnp.where(visible[None], scores, -1e+30)
        row_max = lax.optimization_barrier(jnp.max(scores, axis=-1, keepdims=True))
        weights = jnp.where(visible[None], jnp.exp(scores - row_max), 0.0)
        denominator = lax.optimization_barrier(jnp.sum(weights, axis=-1))
        rounded = lax.optimization_barrier(weights.astype(jnp.bfloat16)).astype(jnp.float32)
        numerator = jnp.einsum('hqk,khd->qhd', rounded, value_rows)
        attention = (numerator / jnp.transpose(denominator)[..., None]).reshape(NEW, D).astype(jnp.bfloat16)
        stream_rows = lax.dynamic_slice_in_dim(stream, index * NEW, NEW, 0)
        normed = layer_norm(stream_rows, norm_gain).astype(jnp.bfloat16)
        gates = lax.dot_general(normed, up_weight, (((1,), (1,)), ((), ())), preferred_element_type=jnp.float32)
        hidden = jax.nn.gelu(gates, approximate=False).astype(jnp.bfloat16)
        summed = jnp.dot(attention, out_weight, preferred_element_type=jnp.float32) + jnp.dot(hidden, down_weight, preferred_element_type=jnp.float32)
        return (stream_rows.astype(jnp.float32) + summed).astype(jnp.bfloat16)
    results = lax.map(one_request, jnp.arange(REQS, dtype=jnp.int32))
    return results.reshape(TOKENS, D)
```

```python
import math

import jax
import jax.numpy as jnp
from jax import lax
from jax.experimental import pallas as pl
from jax.experimental.pallas import tpu as pltpu
from jax.sharding import Mesh, PartitionSpec as P

HD = 256
NORM_EPS = 1e-05
NEG = -(2.0**100)
LOG2E = 1.4426950408889634
SCORE = LOG2E / math.sqrt(HD)
MIB = 1 << 20
F32 = jnp.float32
BF16 = jnp.bfloat16


def ring(step, count):
    return [(i, (i + step) % count) for i in range(count)]


def swap_cores(value):
    return lax.ppermute(value, "c", [(0, 1), (1, 0)])


def params(mib):
    return pltpu.CompilerParams(vmem_limit_bytes=mib * MIB)


def dot(a, b, dims):
    return lax.dot_general(a, b, (dims, ((), ())), preferred_element_type=F32)


def pick_new(place, projections):
    rows, width = projections.shape
    heads = width // (2 * HD)

    def body(place_ref, source, own, other):
        c = place_ref[0]
        for j in range(heads):
            other[:, j * HD : (j + 1) * HD] = source[:, pl.ds((2 * j + 1 - c) * HD, HD)]
        for j in range(heads // 3):
            own[:, j * HD : (j + 1) * HD] = source[:, pl.ds((2 * j + c) * HD, HD)]

    return pl.pallas_call(
        body,
        grid_spec=pltpu.PrefetchScalarGridSpec(
            num_scalar_prefetch=1,
            grid=(1,),
            in_specs=[pl.BlockSpec((rows, width), lambda i, s: (0, 0))],
            out_specs=[
                pl.BlockSpec((rows, width // 6), lambda i, s: (0, 0)),
                pl.BlockSpec((rows, width // 2), lambda i, s: (0, 0)),
            ],
        ),
        out_shape=[
            jax.ShapeDtypeStruct((rows, width // 6), BF16),
            jax.ShapeDtypeStruct((rows, width // 2), BF16),
        ],
        compiler_params=params(16),
        name="pick_new",
    )(place, projections)


def pick_cache(place, cache):
    rows, width = cache.shape
    heads = width // (2 * HD)

    def body(place_ref, source, other):
        other[...] = source[...]

    return pl.pallas_call(
        body,
        grid_spec=pltpu.PrefetchScalarGridSpec(
            num_scalar_prefetch=1,
            grid=(heads,),
            in_specs=[pl.BlockSpec((rows, HD), lambda j, s: (0, 2 * j + 1 - s[0]))],
            out_specs=pl.BlockSpec((rows, HD), lambda j, s: (0, j)),
        ),
        out_shape=jax.ShapeDtypeStruct((rows, width // 2), BF16),
        compiler_params=params(16),
        name="pick_cache",
    )(place, cache)


def norm_kernel(stream, gain, out):
    values = stream[...].astype(F32)
    width = values.shape[1]
    centred = values - jnp.sum(values, axis=-1, keepdims=True) * (1.0 / width)
    spread = jnp.sum(centred * centred, axis=-1, keepdims=True) * (1.0 / width)
    out[...] = (centred * lax.rsqrt(spread + NORM_EPS) * gain[...]).astype(BF16)


def layer_norm(stream, gain):
    return pl.pallas_call(
        norm_kernel,
        out_shape=jax.ShapeDtypeStruct(stream.shape, BF16),
        compiler_params=params(16),
        name="layer_norm",
    )(stream, gain.reshape(1, -1))


def attend_kernel(
    place, ranges, q_ref, k0, k1, v0, v1, nk0, nk1, nv0, nv1, out, stats
):
    j = pl.program_id(0)
    c, z, zq, request = place[0], place[1], place[2], place[3]
    first, end = ranges[request, 0], ranges[request, 1]
    rows = q_ref.shape[0]
    half = rows // 2
    cache_rows = k0.shape[0]
    query = q_ref[...]

    def cached(keys, member):
        position = member * cache_rows + lax.broadcasted_iota(jnp.int32, (1, cache_rows), 1)
        bias = jnp.where((position >= first) & (position < end), 0.0, NEG).astype(F32)
        return dot(query, keys[...], ((1,), (1,))) + bias

    def order(shape, axis):
        place_in = lax.broadcasted_iota(jnp.int32, shape, axis)
        return jnp.where(place_in < half, place_in + c * half, place_in - c * half)

    score_own = cached(k0, 2 * z + c)
    score_other = cached(k1, 2 * z + 1 - c)
    new_keys = jnp.concatenate([nk0[...], nk1[...]], 0)
    new_values = jnp.concatenate([nv0[...], nv1[...]], 0)
    visible = z * rows + order((1, rows), 1) <= zq * rows + order((rows, 1), 0)
    score_new = jnp.where(visible, dot(query, new_keys, ((1,), (1,))), NEG)
    top = jnp.maximum(
        jnp.maximum(
            jnp.max(score_own, axis=-1, keepdims=True),
            jnp.max(score_other, axis=-1, keepdims=True),
        ),
        jnp.max(score_new, axis=-1, keepdims=True),
    )
    shift = top.astype(BF16).astype(F32)

    def weigh(score, values):
        weight = jnp.exp2((score - shift) * SCORE)
        return (
            jnp.sum(weight, axis=-1, keepdims=True),
            dot(weight.astype(BF16), values, ((1,), (0,))),
        )

    parts = [
        weigh(score_own, v0[...]),
        weigh(score_other, v1[...]),
        weigh(score_new, new_values),
    ]
    total = parts[0][0] + parts[1][0] + parts[2][0]
    out[:, pl.ds(pl.multiple_of(j * HD, HD), HD)] = (
        parts[0][1] + parts[1][1] + parts[2][1]
    ).astype(BF16)
    high = total.astype(BF16).astype(F32)
    lane = lax.broadcasted_iota(jnp.int32, stats.shape, 1)
    kept = jnp.where(j == 0, 0.0, stats[...])
    kept = jnp.where(lane == 3 * j, shift, kept)
    kept = jnp.where(lane == 3 * j + 1, high, kept)
    kept = jnp.where(lane == 3 * j + 2, total - high, kept)
    stats[...] = kept
    base = out.shape[1] - stats.shape[1]
    out[:, base:] = kept.astype(BF16)


def attend(place, ranges, query, keys, values, projections, keys_in, values_in, new_in):
    rows, width = query.shape
    heads = width // HD
    cache_rows = keys.shape[0]
    new_rows = projections.shape[0]

    def columns(count, index):
        return pl.BlockSpec((count, HD), index)

    return pl.pallas_call(
        attend_kernel,
        grid_spec=pltpu.PrefetchScalarGridSpec(
            num_scalar_prefetch=2,
            grid=(heads,),
            in_specs=[
                columns(rows, lambda j, s, r: (0, j)),
                columns(cache_rows, lambda j, s, r: (0, 2 * j + s[0])),
                columns(cache_rows, lambda j, s, r: (0, j)),
                columns(cache_rows, lambda j, s, r: (0, 2 * j + s[0])),
                columns(cache_rows, lambda j, s, r: (0, j)),
                columns(new_rows, lambda j, s, r: (0, 2 * heads + 2 * j + s[0])),
                columns(new_rows, lambda j, s, r: (0, heads + j)),
                columns(new_rows, lambda j, s, r: (0, 4 * heads + 2 * j + s[0])),
                columns(new_rows, lambda j, s, r: (0, 2 * heads + j)),
            ],
            out_specs=pl.BlockSpec((rows, width + 128), lambda j, s, r: (0, 0)),
            scratch_shapes=[pltpu.VMEM((rows, 128), F32)],
        ),
        out_shape=jax.ShapeDtypeStruct((rows, width + 128), BF16),
        compiler_params=params(32),
        cost_estimate=pl.CostEstimate(
            flops=4 * rows * (2 * cache_rows + rows) * width,
            transcendentals=rows * (2 * cache_rows + rows) * heads,
            bytes_accessed=8 * cache_rows * width + 8 * rows * width,
        ),
        name="attend",
    )(
        place,
        ranges,
        query,
        keys,
        keys_in,
        values,
        values_in,
        projections,
        new_in,
        projections,
        new_in,
    )


def merge_kernel(place, a, b, c, d, out):
    y = place[4]
    count = out.shape[0]
    parts = (a, b, c, d)
    base = a.shape[1] - 128
    stats = [part[:, base:].astype(F32) for part in parts]
    for j in range(count):
        shifts = [s[:, 3 * j : 3 * j + 1] for s in stats]
        totals = [s[:, 3 * j + 1 : 3 * j + 2] + s[:, 3 * j + 2 : 3 * j + 3] for s in stats]
        top = jnp.maximum(
            jnp.maximum(shifts[0], shifts[1]), jnp.maximum(shifts[2], shifts[3])
        )
        factors = [jnp.exp2((s - top) * SCORE) for s in shifts]
        total = sum(f * t for f, t in zip(factors, totals))
        summed = sum(
            f * part[:, j * HD : (j + 1) * HD].astype(F32) for f, part in zip(factors, parts)
        )
        out[lax.rem(j - y + count, count)] = (summed / total).astype(BF16)


def merge(place, parts):
    rows, width = parts[0].shape
    count = (width - 128) // HD
    whole = pl.BlockSpec((rows, width), lambda i, s: (0, 0))
    return pl.pallas_call(
        merge_kernel,
        grid_spec=pltpu.PrefetchScalarGridSpec(
            num_scalar_prefetch=1,
            grid=(1,),
            in_specs=[whole] * 4,
            out_specs=pl.BlockSpec((count, rows, HD), lambda i, s: (0, 0, 0)),
        ),
        out_shape=jax.ShapeDtypeStruct((count, rows, HD), BF16),
        compiler_params=params(24),
        name="merge",
    )(place, *parts)


def units_kernel(own_in, other_in, attention, weights, out_rows, own, other, total):
    step = pl.program_id(0)
    unit_rows = (weights.shape[1] * 4) // 9
    count = weights.shape[0] * unit_rows
    width = own_in.shape[1]
    rows = own_in.shape[0]

    @pl.when(step == 0)
    def _():
        total[...] = dot(attention[...], out_rows[...], ((1,), (0,)))

    inputs = jnp.concatenate([own_in[...], other_in[...]], 0)
    up = weights[:, :unit_rows, :].reshape(count, width)
    down = weights[:, unit_rows : 2 * unit_rows, :].reshape(count, width)
    gates = dot(inputs, up, ((1,), (1,)))
    hidden = (0.5 * gates * (1.0 + lax.erf(gates * math.sqrt(0.5)))).astype(BF16)
    total[...] += dot(hidden, down, ((1,), (0,)))

    @pl.when(step == pl.num_programs(0) - 1)
    def _():
        own[...] = total[:rows, :]
        other[...] = total[rows:, :].astype(BF16)


def add_units(own_in, other_in, attention, weights, out_rows):
    rows, width = own_in.shape
    shards, shard_rows, _ = weights.shape
    chunk = 4
    return pl.pallas_call(
        units_kernel,
        grid=(shards // chunk,),
        in_specs=[
            pl.BlockSpec((rows, width), lambda i: (0, 0)),
            pl.BlockSpec((rows, width), lambda i: (0, 0)),
            pl.BlockSpec((2 * rows, HD), lambda i: (0, 0)),
            pl.BlockSpec((chunk, shard_rows, width), lambda i: (i, 0, 0)),
            pl.BlockSpec((HD, width), lambda i: (0, 0)),
        ],
        out_specs=[
            pl.BlockSpec((rows, width), lambda i: (0, 0)),
            pl.BlockSpec((rows, width), lambda i: (0, 0)),
        ],
        out_shape=[
            jax.ShapeDtypeStruct((rows, width), F32),
            jax.ShapeDtypeStruct((rows, width), BF16),
        ],
        scratch_shapes=[pltpu.VMEM((2 * rows, width), F32)],
        compiler_params=params(40),
        cost_estimate=pl.CostEstimate(
            flops=2 * 2 * rows * shards * shard_rows * width,
            transcendentals=0,
            bytes_accessed=2 * shards * shard_rows * width + 16 * rows * width,
        ),
        name="units",
    )(own_in, other_in, attention, weights, out_rows)


def on_device(
    stream,
    projections,
    key_cache,
    value_cache,
    cache_range,
    norm_gain,
    out_weight,
    up_weight,
    down_weight,
):
    width = stream.shape[1]
    half = width // 2
    y, x, z, c = (lax.axis_index(name) for name in "yxzc")
    ny, nz = lax.axis_size("y"), lax.axis_size("z")
    request = y * lax.axis_size("x") + x

    weights = lax.all_gather(
        jnp.concatenate([up_weight, down_weight, out_weight], 0), ("x", "z"), axis=0
    )

    def place_of(zq):
        return jnp.stack([c, z, zq, request, y]).astype(jnp.int32)

    place = place_of(z)
    own_query, new_out = pick_new(place, projections)
    new_in = swap_cores(new_out)
    query = jnp.concatenate([own_query, new_in[:, :half]], 0)
    queries = {k: lax.ppermute(query, "z", ring(k, nz)) for k in (2, 1, 3)}
    queries[0] = query
    keys_in = swap_cores(pick_cache(place, key_cache))
    values_in = swap_cores(pick_cache(place, value_cache))

    normed = layer_norm(stream, norm_gain)
    inputs = {k: lax.ppermute(normed, "y", ring(k, ny)) for k in (2, 1, 3)}
    inputs[0] = normed
    others = {k: swap_cores(inputs[k]) for k in (0, 1, 3, 2)}

    partials = {}
    for k in (0, 1, 3, 2):
        made = attend(
            place_of((z - k + nz) % nz),
            cache_range,
            queries[k],
            key_cache,
            value_cache,
            projections,
            keys_in,
            values_in,
            new_in,
        )
        partials[k] = made if k == 0 else lax.ppermute(made, "z", ring(-k, nz))
    heads = merge(place, [partials[k] for k in range(nz)])
    attention = {k: lax.ppermute(heads[k], "y", ring(k, ny)) for k in (2, 1, 3)}
    attention[0] = heads[0]

    shards = weights.shape[0]
    out_shards = weights[:, -out_weight.shape[0] :, :]
    mine = lax.dynamic_slice_in_dim(out_shards, c * (shards // 2), shards // 2, 0)
    theirs = swap_cores(
        lax.dynamic_slice_in_dim(out_shards, (1 - c) * (shards // 2), shards // 2, 0)
    )
    out_rows = jnp.where(
        c == 0, jnp.stack([mine, theirs], 1), jnp.stack([theirs, mine], 1)
    ).reshape(HD, width)

    summed = None
    returned = []
    for k in (2, 1, 3, 0):
        own, other = add_units(inputs[k], others[k], attention[k], weights, out_rows)
        both = own + swap_cores(other).astype(F32)
        if k == 0:
            summed = both
        else:
            returned.append(lax.ppermute(both.astype(BF16), "y", ring(-k, ny)))
    summed = summed + stream.astype(F32)
    for part in returned:
        summed = summed + part.astype(F32)
    return summed.astype(BF16)


def solution(mesh):
    names = ("y", "x", "z", "c")
    requests, others = mesh.devices.shape
    grid = Mesh(mesh.devices.reshape(requests, others // 8, 4, 2), names)
    rows = P(names, None)
    return jax.shard_map(
        on_device,
        mesh=grid,
        in_specs=(rows, rows, rows, rows, P(), P(), rows, rows, rows),
        out_specs=rows,
        check_vma=False,
    )
```

```python
import math

import jax
import jax.numpy as jnp
from jax import lax
from jax.experimental import pallas as pl
from jax.experimental.pallas import tpu as pltpu
from jax.sharding import Mesh, PartitionSpec as P

HD = 256
NORM_EPS = 1e-05
NEG = -(2.0**100)
LOG2E = 1.4426950408889634
SCORE = LOG2E / math.sqrt(HD)
MIB = 1 << 20
F32 = jnp.float32
BF16 = jnp.bfloat16


def ring(step, count):
    return [(i, (i + step) % count) for i in range(count)]


def swap_cores(value):
    return lax.ppermute(value, "c", [(0, 1), (1, 0)])


def params(mib):
    return pltpu.CompilerParams(vmem_limit_bytes=mib * MIB)


def dot(a, b, dims):
    return lax.dot_general(a, b, (dims, ((), ())), preferred_element_type=F32)


def pick_new(place, projections):
    rows, width = projections.shape
    heads = width // (2 * HD)

    def body(place_ref, source, own, other):
        c = place_ref[0]
        for j in range(heads):
            other[:, j * HD : (j + 1) * HD] = source[:, pl.ds((2 * j + 1 - c) * HD, HD)]
        for j in range(heads // 3):
            own[:, j * HD : (j + 1) * HD] = source[:, pl.ds((2 * j + c) * HD, HD)]

    return pl.pallas_call(
        body,
        grid_spec=pltpu.PrefetchScalarGridSpec(
            num_scalar_prefetch=1,
            grid=(1,),
            in_specs=[pl.BlockSpec((rows, width), lambda i, s: (0, 0))],
            out_specs=[
                pl.BlockSpec((rows, width // 6), lambda i, s: (0, 0)),
                pl.BlockSpec((rows, width // 2), lambda i, s: (0, 0)),
            ],
        ),
        out_shape=[
            jax.ShapeDtypeStruct((rows, width // 6), BF16),
            jax.ShapeDtypeStruct((rows, width // 2), BF16),
        ],
        compiler_params=params(16),
        name="pick_new",
    )(place, projections)


def pick_cache(place, cache):
    rows, width = cache.shape
    heads = width // (2 * HD)

    def body(place_ref, source, other):
        other[...] = source[...]

    return pl.pallas_call(
        body,
        grid_spec=pltpu.PrefetchScalarGridSpec(
            num_scalar_prefetch=1,
            grid=(heads,),
            in_specs=[pl.BlockSpec((rows, HD), lambda j, s: (0, 2 * j + 1 - s[0]))],
            out_specs=pl.BlockSpec((rows, HD), lambda j, s: (0, j)),
        ),
        out_shape=jax.ShapeDtypeStruct((rows, width // 2), BF16),
        compiler_params=params(16),
        name="pick_cache",
    )(place, cache)


def norm_kernel(stream, gain, out):
    values = stream[...].astype(F32)
    width = values.shape[1]
    centred = values - jnp.sum(values, axis=-1, keepdims=True) * (1.0 / width)
    spread = jnp.sum(centred * centred, axis=-1, keepdims=True) * (1.0 / width)
    out[...] = (centred * lax.rsqrt(spread + NORM_EPS) * gain[...]).astype(BF16)


def layer_norm(stream, gain):
    return pl.pallas_call(
        norm_kernel,
        out_shape=jax.ShapeDtypeStruct(stream.shape, BF16),
        compiler_params=params(16),
        name="layer_norm",
    )(stream, gain.reshape(1, -1))


def attend_kernel(
    place, ranges, q_ref, k0, k1, v0, v1, nk0, nk1, nv0, nv1, out, stats
):
    j = pl.program_id(0)
    c, z, zq, request = place[0], place[1], place[2], place[3]
    first, end = ranges[request, 0], ranges[request, 1]
    rows = q_ref.shape[0]
    half = rows // 2
    cache_rows = k0.shape[0]
    query = q_ref[...]

    def cached(keys, member):
        position = member * cache_rows + lax.broadcasted_iota(jnp.int32, (1, cache_rows), 1)
        bias = jnp.where((position >= first) & (position < end), 0.0, NEG).astype(F32)
        return dot(query, keys[...], ((1,), (1,))) + bias

    def order(shape, axis):
        place_in = lax.broadcasted_iota(jnp.int32, shape, axis)
        return jnp.where(place_in < half, place_in + c * half, place_in - c * half)

    score_own = cached(k0, 2 * z + c)
    score_other = cached(k1, 2 * z + 1 - c)
    new_keys = jnp.concatenate([nk0[...], nk1[...]], 0)
    new_values = jnp.concatenate([nv0[...], nv1[...]], 0)
    visible = z * rows + order((1, rows), 1) <= zq * rows + order((rows, 1), 0)
    score_new = jnp.where(visible, dot(query, new_keys, ((1,), (1,))), NEG)
    top = jnp.maximum(
        jnp.maximum(
            jnp.max(score_own, axis=-1, keepdims=True),
            jnp.max(score_other, axis=-1, keepdims=True),
        ),
        jnp.max(score_new, axis=-1, keepdims=True),
    )
    shift = top.astype(BF16).astype(F32)

    def weigh(score, values):
        weight = jnp.exp2((score - shift) * SCORE)
        return (
            jnp.sum(weight, axis=-1, keepdims=True),
            dot(weight.astype(BF16), values, ((1,), (0,))),
        )

    parts = [
        weigh(score_own, v0[...]),
        weigh(score_other, v1[...]),
        weigh(score_new, new_values),
    ]
    total = parts[0][0] + parts[1][0] + parts[2][0]
    out[:, pl.ds(pl.multiple_of(j * HD, HD), HD)] = (
        parts[0][1] + parts[1][1] + parts[2][1]
    ).astype(BF16)
    high = total.astype(BF16).astype(F32)
    lane = lax.broadcasted_iota(jnp.int32, stats.shape, 1)
    kept = jnp.where(j == 0, 0.0, stats[...])
    kept = jnp.where(lane == 3 * j, shift, kept)
    kept = jnp.where(lane == 3 * j + 1, high, kept)
    kept = jnp.where(lane == 3 * j + 2, total - high, kept)
    stats[...] = kept
    base = out.shape[1] - stats.shape[1]
    out[:, base:] = kept.astype(BF16)


def attend(place, ranges, query, keys, values, projections, keys_in, values_in, new_in):
    rows, width = query.shape
    heads = width // HD
    cache_rows = keys.shape[0]
    new_rows = projections.shape[0]

    def columns(count, index):
        return pl.BlockSpec((count, HD), index)

    return pl.pallas_call(
        attend_kernel,
        grid_spec=pltpu.PrefetchScalarGridSpec(
            num_scalar_prefetch=2,
            grid=(heads,),
            in_specs=[
                columns(rows, lambda j, s, r: (0, j)),
                columns(cache_rows, lambda j, s, r: (0, 2 * j + s[0])),
                columns(cache_rows, lambda j, s, r: (0, j)),
                columns(cache_rows, lambda j, s, r: (0, 2 * j + s[0])),
                columns(cache_rows, lambda j, s, r: (0, j)),
                columns(new_rows, lambda j, s, r: (0, 2 * heads + 2 * j + s[0])),
                columns(new_rows, lambda j, s, r: (0, heads + j)),
                columns(new_rows, lambda j, s, r: (0, 4 * heads + 2 * j + s[0])),
                columns(new_rows, lambda j, s, r: (0, 2 * heads + j)),
            ],
            out_specs=pl.BlockSpec((rows, width + 128), lambda j, s, r: (0, 0)),
            scratch_shapes=[pltpu.VMEM((rows, 128), F32)],
        ),
        out_shape=jax.ShapeDtypeStruct((rows, width + 128), BF16),
        compiler_params=params(32),
        cost_estimate=pl.CostEstimate(
            flops=4 * rows * (2 * cache_rows + rows) * width,
            transcendentals=rows * (2 * cache_rows + rows) * heads,
            bytes_accessed=8 * cache_rows * width + 8 * rows * width,
        ),
        name="attend",
    )(
        place,
        ranges,
        query,
        keys,
        keys_in,
        values,
        values_in,
        projections,
        new_in,
        projections,
        new_in,
    )


def merge_kernel(place, a, b, c, d, out):
    z = place[1]
    count = out.shape[0]
    parts = (a, b, c, d)
    base = a.shape[1] - 128
    stats = [part[:, base:].astype(F32) for part in parts]
    for j in range(count):
        shifts = [s[:, 3 * j : 3 * j + 1] for s in stats]
        totals = [s[:, 3 * j + 1 : 3 * j + 2] + s[:, 3 * j + 2 : 3 * j + 3] for s in stats]
        top = jnp.maximum(
            jnp.maximum(shifts[0], shifts[1]), jnp.maximum(shifts[2], shifts[3])
        )
        factors = [jnp.exp2((s - top) * SCORE) for s in shifts]
        total = sum(f * t for f, t in zip(factors, totals))
        summed = sum(
            f * part[:, j * HD : (j + 1) * HD].astype(F32) for f, part in zip(factors, parts)
        )
        out[lax.rem(j - z + count, count)] = (summed / total).astype(BF16)


def merge(place, parts):
    rows, width = parts[0].shape
    count = (width - 128) // HD
    whole = pl.BlockSpec((rows, width), lambda i, s: (0, 0))
    return pl.pallas_call(
        merge_kernel,
        grid_spec=pltpu.PrefetchScalarGridSpec(
            num_scalar_prefetch=1,
            grid=(1,),
            in_specs=[whole] * 4,
            out_specs=pl.BlockSpec((count, rows, HD), lambda i, s: (0, 0, 0)),
        ),
        out_shape=jax.ShapeDtypeStruct((count, rows, HD), BF16),
        compiler_params=params(24),
        name="merge",
    )(place, *parts)


def hidden_kernel(own_in, other_in, up_ref, own, other):
    shards, rows, width = up_ref.shape
    up = up_ref[...].reshape(shards * rows, width)
    for inputs, out in ((own_in, own), (other_in, other)):
        gates = dot(inputs[...], up, ((1,), (1,)))
        out[...] = (0.5 * gates * (1.0 + lax.erf(gates * math.sqrt(0.5)))).astype(BF16)


def hidden_units(own_in, other_in, weights, unit_rows):
    rows, width = own_in.shape
    shards = weights.shape[0]
    chunk = 4
    count = chunk * unit_rows
    whole = pl.BlockSpec((rows, width), lambda i: (0, 0))
    part = pl.BlockSpec((rows, count), lambda i: (0, i))
    return pl.pallas_call(
        hidden_kernel,
        grid=(shards // chunk,),
        in_specs=[
            whole,
            whole,
            pl.BlockSpec((chunk, unit_rows, width), lambda i: (i, 0, 0)),
        ],
        out_specs=[part, part],
        out_shape=[jax.ShapeDtypeStruct((rows, shards * unit_rows), BF16)] * 2,
        compiler_params=params(40),
        cost_estimate=pl.CostEstimate(
            flops=4 * rows * shards * unit_rows * width,
            transcendentals=0,
            bytes_accessed=2 * shards * unit_rows * width + 4 * rows * width,
        ),
        name="hidden_units",
    )(own_in, other_in, weights)


def down_kernel(hidden, a0, a1, a2, a3, down_ref, out_ref, *outs):
    shards, rows, columns = down_ref.shape
    down = down_ref[...].reshape(shards * rows, columns)
    out_rows = out_ref[...].reshape(shards * out_ref.shape[1], columns)
    heads = jnp.concatenate([a0[...], a1[...], a2[...], a3[...]], 0)
    made = dot(hidden[...], down, ((1,), (0,))) + dot(heads, out_rows, ((1,), (0,)))
    count = made.shape[0] // len(outs)
    for i, out in enumerate(outs):
        out[...] = made[i * count : (i + 1) * count].astype(out.dtype)


def down_units(hidden, heads, side, weights, unit_rows, dtype):
    rows, units = hidden.shape
    shards, shard_rows, width = weights.shape
    out_rows = shard_rows - 2 * unit_rows
    count = rows // len(heads)
    columns = 512
    return pl.pallas_call(
        down_kernel,
        grid=(width // columns,),
        in_specs=[pl.BlockSpec((rows, units), lambda i: (0, 0))]
        + [pl.BlockSpec((count, HD), lambda i: (side, 0))] * len(heads)
        + [
            pl.BlockSpec((shards, unit_rows, columns), lambda i: (0, 1, i)),
            pl.BlockSpec(
                (shards, out_rows, columns), lambda i: (0, 2 * unit_rows // out_rows, i)
            ),
        ],
        out_specs=[pl.BlockSpec((count, columns), lambda i: (0, i))] * len(heads),
        out_shape=[jax.ShapeDtypeStruct((count, width), dtype)] * len(heads),
        compiler_params=params(40),
        cost_estimate=pl.CostEstimate(
            flops=2 * rows * (units + HD) * width,
            transcendentals=0,
            bytes_accessed=2 * (units + HD) * width + 2 * rows * units + 4 * rows * width,
        ),
        name="down_units",
    )(hidden, *heads, weights, weights)


def head_owners(ny, nx, nz):
    pairs = []
    for y in range(ny):
        for x in range(nx):
            for z in range(nz):
                for c in range(2):
                    place = (x % 2) * 8 + z * 2 + c
                    target = ((place // nx * nx + place % nx) * nz + y) * 2 + x // 2
                    pairs.append((((y * nx + x) * nz + z) * 2 + c, target))
    return pairs


def after(value, *others):
    return lax.optimization_barrier((value, *others))[0]


def on_device(
    stream,
    projections,
    key_cache,
    value_cache,
    cache_range,
    norm_gain,
    out_weight,
    up_weight,
    down_weight,
):
    width = stream.shape[1]
    half = width // 2
    y, x, z, c = (lax.axis_index(name) for name in "yxzc")
    ny, nx, nz = (lax.axis_size(name) for name in "yxz")
    request = y * nx + x
    unit_rows = up_weight.shape[0]

    head_rows = lax.ppermute(out_weight, ("y", "x", "z", "c"), head_owners(ny, nx, nz))
    weights = lax.all_gather(
        jnp.concatenate([up_weight, down_weight, head_rows], 0), ("y", "x"), axis=0
    )

    def place_of(zq):
        return jnp.stack([c, z, zq, request]).astype(jnp.int32)

    place = place_of(z)
    own_query, new_out = pick_new(place, projections)
    new_in = swap_cores(new_out)
    query = jnp.concatenate([own_query, new_in[:, :half]], 0)
    queries = {k: lax.ppermute(query, "z", ring(k, nz)) for k in (2, 1, 3)}
    queries[0] = query
    place_cache = after(place, query)
    keys_in = swap_cores(pick_cache(place_cache, key_cache))
    values_in = swap_cores(pick_cache(place_cache, value_cache))

    made, partials = keys_in, {}
    normed = None
    for k in (0, 1, 3, 2):
        made = attend(
            after(place_of((z - k + nz) % nz), made),
            cache_range,
            queries[k],
            key_cache,
            value_cache,
            projections,
            keys_in,
            values_in,
            new_in,
        )
        partials[k] = made if k == 0 else lax.ppermute(made, "z", ring(-k, nz))
        if k == 0:
            normed = layer_norm(stream, after(norm_gain, made))
    inputs = [normed] + [lax.ppermute(normed, "z", ring(k, nz)) for k in range(1, nz)]
    own_in = jnp.concatenate(inputs, 0)
    other_in = swap_cores(own_in)
    heads = merge(place, [partials[k] for k in range(nz)])
    attention = [heads[0]] + [lax.ppermute(heads[k], "z", ring(k, nz)) for k in range(1, nz)]

    weights = after(weights, heads, other_in)
    own_hidden, other_hidden = hidden_units(own_in, other_in, weights, unit_rows)
    given = down_units(other_hidden, attention, 1, weights, unit_rows, BF16)
    taken = [swap_cores(part) for part in given]
    kept = down_units(own_hidden, attention, 0, after(weights, *given), unit_rows, F32)
    summed = stream.astype(F32) + kept[0] + taken[0].astype(F32)
    for k in (2, 1, 3):
        both = (kept[k] + taken[k].astype(F32)).astype(BF16)
        summed = summed + lax.ppermute(both, "z", ring(-k, nz)).astype(F32)
    return summed.astype(BF16)


def solution(mesh):
    names = ("y", "x", "z", "c")
    requests, others = mesh.devices.shape
    grid = Mesh(mesh.devices.reshape(requests, others // 8, 4, 2), names)
    rows = P(names, None)
    return jax.shard_map(
        on_device,
        mesh=grid,
        in_specs=(rows, rows, rows, rows, P(), P(), rows, rows, rows),
        out_specs=rows,
        check_vma=False,
    )
```

```python
import functools
import math

import jax
import jax.numpy as jnp
from jax import lax
from jax.experimental import pallas as pl
from jax.experimental.pallas import tpu as pltpu
from jax.sharding import Mesh, PartitionSpec as P

HD = 256
NORM_EPS = 1e-05
NEG = -(2.0**100)
LOG2E = 1.4426950408889634
SCORE = LOG2E / math.sqrt(HD)
MIB = 1 << 20
F32 = jnp.float32
BF16 = jnp.bfloat16


def ring(step, count):
    return [(i, (i + step) % count) for i in range(count)]


def swap_cores(value):
    return lax.ppermute(value, "c", [(0, 1), (1, 0)])


def params(mib):
    return pltpu.CompilerParams(vmem_limit_bytes=mib * MIB)


def dot(a, b, dims):
    return lax.dot_general(a, b, (dims, ((), ())), preferred_element_type=F32)


def pick_new(place, projections):
    rows, width = projections.shape
    heads = width // (2 * HD)

    def body(place_ref, source, own, other):
        c = place_ref[0]
        for j in range(heads):
            other[:, j * HD : (j + 1) * HD] = source[:, pl.ds((2 * j + 1 - c) * HD, HD)]
        for j in range(heads // 3):
            own[:, j * HD : (j + 1) * HD] = source[:, pl.ds((2 * j + c) * HD, HD)]

    return pl.pallas_call(
        body,
        grid_spec=pltpu.PrefetchScalarGridSpec(
            num_scalar_prefetch=1,
            grid=(1,),
            in_specs=[pl.BlockSpec((rows, width), lambda i, s: (0, 0))],
            out_specs=[
                pl.BlockSpec((rows, width // 6), lambda i, s: (0, 0)),
                pl.BlockSpec((rows, width // 2), lambda i, s: (0, 0)),
            ],
        ),
        out_shape=[
            jax.ShapeDtypeStruct((rows, width // 6), BF16),
            jax.ShapeDtypeStruct((rows, width // 2), BF16),
        ],
        compiler_params=params(16),
        name="pick_new",
    )(place, projections)


def pick_cache(place, keys, values):
    rows, width = keys.shape
    heads = width // (2 * HD)

    def body(place_ref, key_ref, value_ref, other, arrived):
        c = place_ref[0]
        copies = []
        for i, source in enumerate((key_ref, value_ref)):
            for j in range(heads):
                start = pl.multiple_of((2 * j + 1 - c) * HD, HD)
                copies.append(
                    pltpu.make_async_copy(
                        source.at[:, pl.ds(start, HD)],
                        other.at[i, :, pl.ds(j * HD, HD)],
                        arrived.at[i * heads + j],
                    )
                )
        for copy in copies:
            copy.start()
        for copy in copies:
            copy.wait()

    whole = pl.BlockSpec(memory_space=pl.ANY)
    return pl.pallas_call(
        body,
        grid_spec=pltpu.PrefetchScalarGridSpec(
            num_scalar_prefetch=1,
            grid=(1,),
            in_specs=[whole, whole],
            out_specs=whole,
            scratch_shapes=[pltpu.SemaphoreType.DMA((2 * heads,))],
        ),
        out_shape=jax.ShapeDtypeStruct((2, rows, width // 2), BF16),
        compiler_params=params(16),
        name="pick_cache",
    )(place, keys, values)


def norm_kernel(stream, gain, out):
    values = stream[...].astype(F32)
    width = values.shape[1]
    centred = values - jnp.sum(values, axis=-1, keepdims=True) * (1.0 / width)
    spread = jnp.sum(centred * centred, axis=-1, keepdims=True) * (1.0 / width)
    out[...] = (centred * lax.rsqrt(spread + NORM_EPS) * gain[...]).astype(BF16)


def layer_norm(stream, gain):
    return pl.pallas_call(
        norm_kernel,
        out_shape=jax.ShapeDtypeStruct(stream.shape, BF16),
        compiler_params=params(16),
        name="layer_norm",
    )(stream, gain.reshape(1, -1))


def attend_kernel(steps, place, ranges, *refs):
    blocks = len(steps)
    queries, refs = refs[:blocks], refs[blocks:]
    k0, k1, v0, v1, nk0, nk1, nv0, nv1 = refs[:8]
    outs, stats = refs[8 : 8 + blocks], refs[8 + blocks]
    j = pl.program_id(0)
    c, z, request = place[0], place[1], place[2]
    first, end = ranges[request, 0], ranges[request, 1]
    rows = queries[0].shape[0]
    half = rows // 2
    cache_rows = k0.shape[0]
    lane = lax.broadcasted_iota(jnp.int32, stats.shape[1:], 1)

    def bias(member):
        position = member * cache_rows + lax.broadcasted_iota(jnp.int32, (1, cache_rows), 1)
        return jnp.where((position >= first) & (position < end), 0.0, NEG).astype(F32)

    def order(shape, axis):
        place_in = lax.broadcasted_iota(jnp.int32, shape, axis)
        return jnp.where(place_in < half, place_in + c * half, place_in - c * half)

    bias_own, bias_other = bias(2 * z + c), bias(2 * z + 1 - c)
    new_keys = jnp.concatenate([nk0[...], nk1[...]], 0)
    new_values = jnp.concatenate([nv0[...], nv1[...]], 0)
    for i, (step, out) in enumerate(zip(steps, outs)):
        zq = lax.rem(z - step + 4, 4)
        query = queries[i][...]
        score_own = dot(query, k0[...], ((1,), (1,))) + bias_own
        score_other = dot(query, k1[...], ((1,), (1,))) + bias_other
        visible = z * rows + order((1, rows), 1) <= zq * rows + order((rows, 1), 0)
        score_new = jnp.where(visible, dot(query, new_keys, ((1,), (1,))), NEG)
        top = jnp.maximum(
            jnp.maximum(
                jnp.max(score_own, axis=-1, keepdims=True),
                jnp.max(score_other, axis=-1, keepdims=True),
            ),
            jnp.max(score_new, axis=-1, keepdims=True),
        )
        shift = top.astype(BF16).astype(F32)

        def weigh(score, values):
            weight = jnp.exp2((score - shift) * SCORE)
            return (
                jnp.sum(weight, axis=-1, keepdims=True),
                dot(weight.astype(BF16), values, ((1,), (0,))),
            )

        parts = [
            weigh(score_own, v0[...]),
            weigh(score_other, v1[...]),
            weigh(score_new, new_values),
        ]
        total = parts[0][0] + parts[1][0] + parts[2][0]
        out[:, pl.ds(pl.multiple_of(j * HD, HD), HD)] = (
            parts[0][1] + parts[1][1] + parts[2][1]
        ).astype(BF16)
        high = total.astype(BF16).astype(F32)
        kept = jnp.where(j == 0, 0.0, stats[i])
        kept = jnp.where(lane == 3 * j, shift, kept)
        kept = jnp.where(lane == 3 * j + 1, high, kept)
        kept = jnp.where(lane == 3 * j + 2, total - high, kept)
        stats[i] = kept
        out[:, out.shape[1] - 128 :] = kept.astype(BF16)


def attend(steps, place, ranges, queries, keys, values, projections, cache_in, new_in):
    rows, width = queries[0].shape
    blocks = len(steps)
    heads = width // HD
    cache_rows = keys.shape[0]
    new_rows = projections.shape[0]

    def columns(count, index):
        return pl.BlockSpec((count, HD), index)

    def received(i):
        return pl.BlockSpec((None, cache_rows, HD), lambda j, s, r: (i, 0, j))

    return pl.pallas_call(
        functools.partial(attend_kernel, steps),
        grid_spec=pltpu.PrefetchScalarGridSpec(
            num_scalar_prefetch=2,
            grid=(heads,),
            in_specs=[columns(rows, lambda j, s, r: (0, j))] * blocks
            + [
                columns(cache_rows, lambda j, s, r: (0, 2 * j + s[0])),
                received(0),
                columns(cache_rows, lambda j, s, r: (0, 2 * j + s[0])),
                received(1),
                columns(new_rows, lambda j, s, r: (0, 2 * heads + 2 * j + s[0])),
                columns(new_rows, lambda j, s, r: (0, heads + j)),
                columns(new_rows, lambda j, s, r: (0, 4 * heads + 2 * j + s[0])),
                columns(new_rows, lambda j, s, r: (0, 2 * heads + j)),
            ],
            out_specs=[pl.BlockSpec((rows, width + 128), lambda j, s, r: (0, 0))] * blocks,
            scratch_shapes=[pltpu.VMEM((blocks, rows, 128), F32)],
        ),
        out_shape=[jax.ShapeDtypeStruct((rows, width + 128), BF16)] * blocks,
        compiler_params=params(40),
        cost_estimate=pl.CostEstimate(
            flops=4 * blocks * rows * (2 * cache_rows + rows) * width,
            transcendentals=blocks * rows * (2 * cache_rows + rows) * heads,
            bytes_accessed=8 * cache_rows * width + 8 * blocks * rows * width,
        ),
        name="attend",
    )(
        place,
        ranges,
        *queries,
        keys,
        cache_in,
        values,
        cache_in,
        projections,
        new_in,
        projections,
        new_in,
    )


def merge_kernel(place, a, b, c, d, out):
    z = place[1]
    count = out.shape[0]
    parts = (a, b, c, d)
    base = a.shape[1] - 128
    stats = [part[:, base:].astype(F32) for part in parts]
    for j in range(count):
        shifts = [s[:, 3 * j : 3 * j + 1] for s in stats]
        totals = [s[:, 3 * j + 1 : 3 * j + 2] + s[:, 3 * j + 2 : 3 * j + 3] for s in stats]
        top = jnp.maximum(
            jnp.maximum(shifts[0], shifts[1]), jnp.maximum(shifts[2], shifts[3])
        )
        factors = [jnp.exp2((s - top) * SCORE) for s in shifts]
        total = sum(f * t for f, t in zip(factors, totals))
        summed = sum(
            f * part[:, j * HD : (j + 1) * HD].astype(F32) for f, part in zip(factors, parts)
        )
        out[lax.rem(j - z + count, count)] = (summed / total).astype(BF16)


def merge(place, parts):
    rows, width = parts[0].shape
    count = (width - 128) // HD
    whole = pl.BlockSpec((rows, width), lambda i, s: (0, 0))
    return pl.pallas_call(
        merge_kernel,
        grid_spec=pltpu.PrefetchScalarGridSpec(
            num_scalar_prefetch=1,
            grid=(1,),
            in_specs=[whole] * 4,
            out_specs=pl.BlockSpec((count, rows, HD), lambda i, s: (0, 0, 0)),
        ),
        out_shape=jax.ShapeDtypeStruct((count, rows, HD), BF16),
        compiler_params=params(24),
        name="merge",
    )(place, *parts)


def hidden_kernel(own_in, other_in, up_ref, own, other):
    shards, rows, width = up_ref.shape
    up = up_ref[...].reshape(shards * rows, width)
    for inputs, out in ((own_in, own), (other_in, other)):
        gates = dot(inputs[...], up, ((1,), (1,)))
        out[...] = (0.5 * gates * (1.0 + lax.erf(gates * math.sqrt(0.5)))).astype(BF16)


def hidden_units(own_in, other_in, weights, unit_rows):
    rows, width = own_in.shape
    shards = weights.shape[0]
    chunk = 4
    count = chunk * unit_rows
    whole = pl.BlockSpec((rows, width), lambda i: (0, 0))
    part = pl.BlockSpec((rows, count), lambda i: (0, i))
    return pl.pallas_call(
        hidden_kernel,
        grid=(shards // chunk,),
        in_specs=[
            whole,
            whole,
            pl.BlockSpec((chunk, unit_rows, width), lambda i: (i, 0, 0)),
        ],
        out_specs=[part, part],
        out_shape=[jax.ShapeDtypeStruct((rows, shards * unit_rows), BF16)] * 2,
        compiler_params=params(40),
        cost_estimate=pl.CostEstimate(
            flops=4 * rows * shards * unit_rows * width,
            transcendentals=0,
            bytes_accessed=2 * shards * unit_rows * width + 4 * rows * width,
        ),
        name="hidden_units",
    )(own_in, other_in, weights)


def down_kernel(hidden, a0, a1, a2, a3, down_ref, out_ref, *outs):
    shards, rows, columns = down_ref.shape
    down = down_ref[...].reshape(shards * rows, columns)
    out_rows = out_ref[...].reshape(shards * out_ref.shape[1], columns)
    heads = jnp.concatenate([a0[...], a1[...], a2[...], a3[...]], 0)
    made = dot(hidden[...], down, ((1,), (0,))) + dot(heads, out_rows, ((1,), (0,)))
    count = made.shape[0] // len(outs)
    for i, out in enumerate(outs):
        out[...] = made[i * count : (i + 1) * count].astype(out.dtype)


def down_units(hidden, heads, side, weights, unit_rows, dtype):
    rows, units = hidden.shape
    shards, shard_rows, width = weights.shape
    out_rows = shard_rows - 2 * unit_rows
    count = rows // len(heads)
    columns = 512
    return pl.pallas_call(
        down_kernel,
        grid=(width // columns,),
        in_specs=[pl.BlockSpec((rows, units), lambda i: (0, 0))]
        + [pl.BlockSpec((count, HD), lambda i: (side, 0))] * len(heads)
        + [
            pl.BlockSpec((shards, unit_rows, columns), lambda i: (0, 1, i)),
            pl.BlockSpec(
                (shards, out_rows, columns), lambda i: (0, 2 * unit_rows // out_rows, i)
            ),
        ],
        out_specs=[pl.BlockSpec((count, columns), lambda i: (0, i))] * len(heads),
        out_shape=[jax.ShapeDtypeStruct((count, width), dtype)] * len(heads),
        compiler_params=params(40),
        cost_estimate=pl.CostEstimate(
            flops=2 * rows * (units + HD) * width,
            transcendentals=0,
            bytes_accessed=2 * (units + HD) * width + 2 * rows * units + 4 * rows * width,
        ),
        name="down_units",
    )(hidden, *heads, weights, weights)


def head_owners(ny, nx, nz):
    pairs = []
    for y in range(ny):
        for x in range(nx):
            for z in range(nz):
                for c in range(2):
                    place = (x % 2) * 8 + z * 2 + c
                    target = ((place // nx * nx + place % nx) * nz + y) * 2 + x // 2
                    pairs.append((((y * nx + x) * nz + z) * 2 + c, target))
    return pairs


def after(value, *others):
    return lax.optimization_barrier((value, *others))[0]


def on_device(
    stream,
    projections,
    key_cache,
    value_cache,
    cache_range,
    norm_gain,
    out_weight,
    up_weight,
    down_weight,
):
    width = stream.shape[1]
    half = width // 2
    y, x, z, c = (lax.axis_index(name) for name in "yxzc")
    ny, nx, nz = (lax.axis_size(name) for name in "yxz")
    request = y * nx + x
    unit_rows = up_weight.shape[0]

    head_rows = lax.ppermute(out_weight, ("y", "x", "z", "c"), head_owners(ny, nx, nz))
    weights = lax.all_gather(
        jnp.concatenate([up_weight, down_weight, head_rows], 0), ("y", "x"), axis=0
    )

    place = jnp.stack([c, z, request]).astype(jnp.int32)
    own_query, new_out = pick_new(place, projections)
    new_in = swap_cores(new_out)
    query = jnp.concatenate([own_query, new_in[:, :half]], 0)
    queries = [lax.ppermute(query, "z", ring(k, nz)) for k in (2, 1, 3)]
    cache_in = swap_cores(pick_cache(after(place, query), key_cache, value_cache))
    context = (key_cache, value_cache, projections, cache_in, new_in)
    (partial,) = attend((0,), place, cache_range, [query], *context)

    norm_gain, place_late = after((norm_gain, place), partial, *queries)
    normed = layer_norm(stream, norm_gain)
    place_late = after(place_late, normed)
    sent = attend((2, 1, 3), place_late, cache_range, queries, *context)
    inputs = [normed] + [lax.ppermute(normed, "z", ring(k, nz)) for k in range(1, nz)]
    sent, inputs = lax.optimization_barrier((sent, inputs))
    partials = [partial] + [
        lax.ppermute(made, "z", ring(-k, nz)) for k, made in zip((2, 1, 3), sent)
    ]
    own_in = jnp.concatenate(inputs, 0)
    other_in = swap_cores(own_in)
    heads = merge(place, partials)
    attention = [heads[0]] + [lax.ppermute(heads[k], "z", ring(k, nz)) for k in range(1, nz)]

    weights = after(weights, heads, other_in)
    own_hidden, other_hidden = hidden_units(own_in, other_in, weights, unit_rows)
    given = down_units(other_hidden, attention, 1, weights, unit_rows, BF16)
    taken = [swap_cores(part) for part in given]
    kept = down_units(own_hidden, attention, 0, after(weights, *given), unit_rows, F32)
    summed = stream.astype(F32) + kept[0] + taken[0].astype(F32)
    for k in (2, 1, 3):
        both = (kept[k] + taken[k].astype(F32)).astype(BF16)
        summed = summed + lax.ppermute(both, "z", ring(-k, nz)).astype(F32)
    return summed.astype(BF16)


def solution(mesh):
    names = ("y", "x", "z", "c")
    requests, others = mesh.devices.shape
    grid = Mesh(mesh.devices.reshape(requests, others // 8, 4, 2), names)
    rows = P(names, None)
    return jax.shard_map(
        on_device,
        mesh=grid,
        in_specs=(rows, rows, rows, rows, P(), P(), rows, rows, rows),
        out_specs=rows,
        check_vma=False,
    )
```

```python
import functools
import math

import jax
import jax.numpy as jnp
from jax import lax
from jax.experimental import pallas as pl
from jax.experimental.pallas import tpu as pltpu
from jax.sharding import Mesh, PartitionSpec as P

HD = 256
NORM_EPS = 1e-05
NEG = -(2.0**100)
LOG2E = 1.4426950408889634
SCORE = LOG2E / math.sqrt(HD)
MIB = 1 << 20
F32 = jnp.float32
BF16 = jnp.bfloat16


def ring(step, count):
    return [(i, (i + step) % count) for i in range(count)]


def swap_cores(value):
    return lax.ppermute(value, "c", [(0, 1), (1, 0)])


def params(mib):
    return pltpu.CompilerParams(vmem_limit_bytes=mib * MIB)


def dot(a, b, dims):
    return lax.dot_general(a, b, (dims, ((), ())), preferred_element_type=F32)


def pick_new(place, projections):
    rows, width = projections.shape
    heads = width // (2 * HD)

    def body(place_ref, source, own, other):
        c = place_ref[0]
        for j in range(heads):
            other[:, j * HD : (j + 1) * HD] = source[:, pl.ds((2 * j + 1 - c) * HD, HD)]
        for j in range(heads // 3):
            own[:, j * HD : (j + 1) * HD] = source[:, pl.ds((2 * j + c) * HD, HD)]

    return pl.pallas_call(
        body,
        grid_spec=pltpu.PrefetchScalarGridSpec(
            num_scalar_prefetch=1,
            grid=(1,),
            in_specs=[pl.BlockSpec((rows, width), lambda i, s: (0, 0))],
            out_specs=[
                pl.BlockSpec((rows, width // 6), lambda i, s: (0, 0)),
                pl.BlockSpec((rows, width // 2), lambda i, s: (0, 0)),
            ],
        ),
        out_shape=[
            jax.ShapeDtypeStruct((rows, width // 6), BF16),
            jax.ShapeDtypeStruct((rows, width // 2), BF16),
        ],
        compiler_params=params(16),
        name="pick_new",
    )(place, projections)


def pick_cache(place, keys, values):
    rows, width = keys.shape
    heads = width // (2 * HD)

    def body(place_ref, key_ref, value_ref, other, held, arrived, left):
        c = place_ref[0]
        copies = []
        for i, source in enumerate((key_ref, value_ref)):
            for j in range(heads):
                start = pl.multiple_of((2 * j + 1 - c) * HD, HD)
                columns = pl.ds(j * HD, HD)
                slot = held.at[i, :, columns]
                copies.append(
                    (
                        pltpu.make_async_copy(
                            source.at[:, pl.ds(start, HD)], slot, arrived.at[i * heads + j]
                        ),
                        pltpu.make_async_copy(
                            slot, other.at[i, :, columns], left.at[i * heads + j]
                        ),
                    )
                )
        for come, _ in copies:
            come.start()
        for come, leave in copies:
            come.wait()
            leave.start()
        for _, leave in copies:
            leave.wait()

    whole = pl.BlockSpec(memory_space=pl.ANY)
    return pl.pallas_call(
        body,
        grid_spec=pltpu.PrefetchScalarGridSpec(
            num_scalar_prefetch=1,
            grid=(1,),
            in_specs=[whole, whole],
            out_specs=pl.BlockSpec(memory_space=pltpu.HBM),
            scratch_shapes=[
                pltpu.VMEM((2, rows, width // 2), BF16),
                pltpu.SemaphoreType.DMA((2 * heads,)),
                pltpu.SemaphoreType.DMA((2 * heads,)),
            ],
        ),
        out_shape=jax.ShapeDtypeStruct((2, rows, width // 2), BF16),
        compiler_params=params(16),
        name="pick_cache",
    )(place, keys, values)


def norm_kernel(stream, gain, out):
    values = stream[...].astype(F32)
    width = values.shape[1]
    centred = values - jnp.sum(values, axis=-1, keepdims=True) * (1.0 / width)
    spread = jnp.sum(centred * centred, axis=-1, keepdims=True) * (1.0 / width)
    out[...] = (centred * lax.rsqrt(spread + NORM_EPS) * gain[...]).astype(BF16)


def layer_norm(stream, gain):
    return pl.pallas_call(
        norm_kernel,
        out_shape=jax.ShapeDtypeStruct(stream.shape, BF16),
        compiler_params=params(16),
        name="layer_norm",
    )(stream, gain.reshape(1, -1))


def attend_kernel(steps, place, ranges, *refs):
    blocks = len(steps)
    queries, refs = refs[:blocks], refs[blocks:]
    k0, k1, v0, v1, nk0, nk1, nv0, nv1 = refs[:8]
    outs, stats = refs[8 : 8 + blocks], refs[8 + blocks]
    j = pl.program_id(0)
    c, z, request = place[0], place[1], place[2]
    first, end = ranges[request, 0], ranges[request, 1]
    rows = queries[0].shape[0]
    half = rows // 2
    cache_rows = k0.shape[0]
    lane = lax.broadcasted_iota(jnp.int32, stats.shape[1:], 1)

    def bias(member):
        position = member * cache_rows + lax.broadcasted_iota(jnp.int32, (1, cache_rows), 1)
        return jnp.where((position >= first) & (position < end), 0.0, NEG).astype(F32)

    def order(shape, axis):
        place_in = lax.broadcasted_iota(jnp.int32, shape, axis)
        return jnp.where(place_in < half, place_in + c * half, place_in - c * half)

    bias_own, bias_other = bias(2 * z + c), bias(2 * z + 1 - c)
    new_keys = jnp.concatenate([nk0[...], nk1[...]], 0)
    new_values = jnp.concatenate([nv0[...], nv1[...]], 0)
    for i, (step, out) in enumerate(zip(steps, outs)):
        zq = lax.rem(z - step + 4, 4)
        query = queries[i][...]
        score_own = dot(query, k0[...], ((1,), (1,))) + bias_own
        score_other = dot(query, k1[...], ((1,), (1,))) + bias_other
        visible = z * rows + order((1, rows), 1) <= zq * rows + order((rows, 1), 0)
        score_new = jnp.where(visible, dot(query, new_keys, ((1,), (1,))), NEG)
        top = jnp.maximum(
            jnp.maximum(
                jnp.max(score_own, axis=-1, keepdims=True),
                jnp.max(score_other, axis=-1, keepdims=True),
            ),
            jnp.max(score_new, axis=-1, keepdims=True),
        )
        shift = top.astype(BF16).astype(F32)

        def weigh(score, values):
            weight = jnp.exp2((score - shift) * SCORE)
            return (
                jnp.sum(weight, axis=-1, keepdims=True),
                dot(weight.astype(BF16), values, ((1,), (0,))),
            )

        parts = [
            weigh(score_own, v0[...]),
            weigh(score_other, v1[...]),
            weigh(score_new, new_values),
        ]
        total = parts[0][0] + parts[1][0] + parts[2][0]
        out[:, pl.ds(pl.multiple_of(j * HD, HD), HD)] = (
            parts[0][1] + parts[1][1] + parts[2][1]
        ).astype(BF16)
        high = total.astype(BF16).astype(F32)
        kept = jnp.where(j == 0, 0.0, stats[i])
        kept = jnp.where(lane == 3 * j, shift, kept)
        kept = jnp.where(lane == 3 * j + 1, high, kept)
        kept = jnp.where(lane == 3 * j + 2, total - high, kept)
        stats[i] = kept
        out[:, out.shape[1] - 128 :] = kept.astype(BF16)


def attend(steps, place, ranges, queries, keys, values, projections, cache_in, new_in):
    rows, width = queries[0].shape
    blocks = len(steps)
    heads = width // HD
    cache_rows = keys.shape[0]
    new_rows = projections.shape[0]

    def columns(count, index):
        return pl.BlockSpec((count, HD), index)

    def received(i):
        return pl.BlockSpec((None, cache_rows, HD), lambda j, s, r: (i, 0, j))

    return pl.pallas_call(
        functools.partial(attend_kernel, steps),
        grid_spec=pltpu.PrefetchScalarGridSpec(
            num_scalar_prefetch=2,
            grid=(heads,),
            in_specs=[columns(rows, lambda j, s, r: (0, j))] * blocks
            + [
                columns(cache_rows, lambda j, s, r: (0, 2 * j + s[0])),
                received(0),
                columns(cache_rows, lambda j, s, r: (0, 2 * j + s[0])),
                received(1),
                columns(new_rows, lambda j, s, r: (0, 2 * heads + 2 * j + s[0])),
                columns(new_rows, lambda j, s, r: (0, heads + j)),
                columns(new_rows, lambda j, s, r: (0, 4 * heads + 2 * j + s[0])),
                columns(new_rows, lambda j, s, r: (0, 2 * heads + j)),
            ],
            out_specs=[pl.BlockSpec((rows, width + 128), lambda j, s, r: (0, 0))] * blocks,
            scratch_shapes=[pltpu.VMEM((blocks, rows, 128), F32)],
        ),
        out_shape=[jax.ShapeDtypeStruct((rows, width + 128), BF16)] * blocks,
        compiler_params=params(40),
        cost_estimate=pl.CostEstimate(
            flops=4 * blocks * rows * (2 * cache_rows + rows) * width,
            transcendentals=blocks * rows * (2 * cache_rows + rows) * heads,
            bytes_accessed=8 * cache_rows * width + 8 * blocks * rows * width,
        ),
        name="attend",
    )(
        place,
        ranges,
        *queries,
        keys,
        cache_in,
        values,
        cache_in,
        projections,
        new_in,
        projections,
        new_in,
    )


def merge_kernel(place, a, b, c, d, out):
    z = place[1]
    count = out.shape[0]
    parts = (a, b, c, d)
    base = a.shape[1] - 128
    stats = [part[:, base:].astype(F32) for part in parts]
    for j in range(count):
        shifts = [s[:, 3 * j : 3 * j + 1] for s in stats]
        totals = [s[:, 3 * j + 1 : 3 * j + 2] + s[:, 3 * j + 2 : 3 * j + 3] for s in stats]
        top = jnp.maximum(
            jnp.maximum(shifts[0], shifts[1]), jnp.maximum(shifts[2], shifts[3])
        )
        factors = [jnp.exp2((s - top) * SCORE) for s in shifts]
        total = sum(f * t for f, t in zip(factors, totals))
        summed = sum(
            f * part[:, j * HD : (j + 1) * HD].astype(F32) for f, part in zip(factors, parts)
        )
        out[lax.rem(j - z + count, count)] = (summed / total).astype(BF16)


def merge(place, parts):
    rows, width = parts[0].shape
    count = (width - 128) // HD
    whole = pl.BlockSpec((rows, width), lambda i, s: (0, 0))
    return pl.pallas_call(
        merge_kernel,
        grid_spec=pltpu.PrefetchScalarGridSpec(
            num_scalar_prefetch=1,
            grid=(1,),
            in_specs=[whole] * 4,
            out_specs=pl.BlockSpec((count, rows, HD), lambda i, s: (0, 0, 0)),
        ),
        out_shape=jax.ShapeDtypeStruct((count, rows, HD), BF16),
        compiler_params=params(12),
        name="merge",
    )(place, *parts)


def hidden_kernel(own_in, other_in, up_ref, own, other):
    shards, rows, width = up_ref.shape
    up = up_ref[...].reshape(shards * rows, width)
    for inputs, out in ((own_in, own), (other_in, other)):
        gates = dot(inputs[...], up, ((1,), (1,)))
        out[...] = (0.5 * gates * (1.0 + lax.erf(gates * math.sqrt(0.5)))).astype(BF16)


def hidden_units(own_in, other_in, weights, unit_rows):
    rows, width = own_in.shape
    shards = weights.shape[0]
    chunk = 4
    count = chunk * unit_rows
    whole = pl.BlockSpec((rows, width), lambda i: (0, 0))
    part = pl.BlockSpec((rows, count), lambda i: (0, i))
    return pl.pallas_call(
        hidden_kernel,
        grid=(shards // chunk,),
        in_specs=[
            whole,
            whole,
            pl.BlockSpec((chunk, unit_rows, width), lambda i: (i, 0, 0)),
        ],
        out_specs=[part, part],
        out_shape=[jax.ShapeDtypeStruct((rows, shards * unit_rows), BF16)] * 2,
        compiler_params=params(20),
        cost_estimate=pl.CostEstimate(
            flops=4 * rows * shards * unit_rows * width,
            transcendentals=0,
            bytes_accessed=2 * shards * unit_rows * width + 4 * rows * width,
        ),
        name="hidden_units",
    )(own_in, other_in, weights)


def down_kernel(own_hidden, other_hidden, down_ref, own, other):
    shards, rows, columns = down_ref.shape
    down = down_ref[...].reshape(shards * rows, columns)
    other[...] = dot(other_hidden[...], down, ((1,), (0,)))
    own[...] = dot(own_hidden[...], down, ((1,), (0,)))


def down_units(own_hidden, other_hidden, weights, unit_rows):
    rows, units = own_hidden.shape
    shards, _, width = weights.shape
    columns = 512
    whole = pl.BlockSpec((rows, units), lambda i: (0, 0))
    part = pl.BlockSpec((rows, columns), lambda i: (0, i))
    return pl.pallas_call(
        down_kernel,
        grid=(width // columns,),
        in_specs=[
            whole,
            whole,
            pl.BlockSpec((shards, unit_rows, columns), lambda i: (0, 1, i)),
        ],
        out_specs=[part, part],
        out_shape=[jax.ShapeDtypeStruct((rows, width), F32)] * 2,
        compiler_params=params(20),
        cost_estimate=pl.CostEstimate(
            flops=4 * rows * units * width,
            transcendentals=0,
            bytes_accessed=2 * units * width + 4 * rows * units + 8 * rows * width,
        ),
        name="down_units",
    )(own_hidden, other_hidden, weights)


def finish_kernel(partial, a0, a1, a2, a3, out_ref, *outs):
    shards, rows, columns = out_ref.shape
    heads = jnp.concatenate([a0[...], a1[...], a2[...], a3[...]], 0)
    out_rows = out_ref[...].reshape(shards * rows, columns)
    made = partial[...] + dot(heads, out_rows, ((1,), (0,)))
    count = made.shape[0] // len(outs)
    for i, out in enumerate(outs):
        out[...] = made[i * count : (i + 1) * count].astype(out.dtype)


def finish(partial, heads, side, weights, unit_rows, dtype):
    rows, width = partial.shape
    shards, shard_rows, _ = weights.shape
    out_rows = shard_rows - 2 * unit_rows
    count = rows // len(heads)
    columns = 512
    return pl.pallas_call(
        finish_kernel,
        grid=(width // columns,),
        in_specs=[pl.BlockSpec((rows, columns), lambda i: (0, i))]
        + [pl.BlockSpec((count, HD), lambda i: (side, 0))] * len(heads)
        + [
            pl.BlockSpec(
                (shards, out_rows, columns), lambda i: (0, 2 * unit_rows // out_rows, i)
            ),
        ],
        out_specs=[pl.BlockSpec((count, columns), lambda i: (0, i))] * len(heads),
        out_shape=[jax.ShapeDtypeStruct((count, width), dtype)] * len(heads),
        compiler_params=params(16),
        cost_estimate=pl.CostEstimate(
            flops=2 * rows * HD * width,
            transcendentals=0,
            bytes_accessed=2 * HD * width + 8 * rows * width,
        ),
        name="finish",
    )(partial, *heads, weights)


def head_owners(ny, nx, nz):
    pairs = []
    for y in range(ny):
        for x in range(nx):
            for z in range(nz):
                for c in range(2):
                    place = (x % 2) * 8 + z * 2 + c
                    target = ((place // nx * nx + place % nx) * nz + y) * 2 + x // 2
                    pairs.append((((y * nx + x) * nz + z) * 2 + c, target))
    return pairs


def in_hbm(*arrays):
    return tuple(pltpu.with_memory_space_constraint(array, pltpu.HBM) for array in arrays)


def after(value, *others):
    return lax.optimization_barrier((value, *others))[0]


def on_device(
    stream,
    projections,
    key_cache,
    value_cache,
    cache_range,
    norm_gain,
    out_weight,
    up_weight,
    down_weight,
):
    width = stream.shape[1]
    half = width // 2
    y, x, z, c = (lax.axis_index(name) for name in "yxzc")
    ny, nx, nz = (lax.axis_size(name) for name in "yxz")
    request = y * nx + x
    unit_rows = up_weight.shape[0]

    place = jnp.stack([c, z, request]).astype(jnp.int32)
    head_rows = lax.ppermute(out_weight, ("y", "x", "z", "c"), head_owners(ny, nx, nz))
    cached = in_hbm(key_cache, value_cache)
    own_query, new_out = pick_new(place, projections)
    new_in = swap_cores(new_out)
    (cache_out,) = in_hbm(pick_cache(after(place, new_out), *cached))
    head_rows = after(head_rows, cache_out)
    weights = lax.all_gather(
        jnp.concatenate([up_weight, down_weight, head_rows], 0), ("y", "x"), axis=0
    )
    query = jnp.concatenate([own_query, new_in[:, :half]], 0)
    queries = [lax.ppermute(query, "z", ring(k, nz)) for k in (2, 1, 3)]
    cache_in = swap_cores(after(cache_out, query))
    context = (*cached, *in_hbm(projections), cache_in, new_in)
    (partial,) = attend((0,), place, cache_range, [query], *context)

    norm_gain, place_late = after((norm_gain, place), partial, *queries)
    normed = layer_norm(stream, norm_gain)
    place_late = after(place_late, normed)
    sent = attend((2, 1, 3), place_late, cache_range, queries, *context)
    inputs = [normed] + [lax.ppermute(normed, "z", ring(k, nz)) for k in range(1, nz)]
    sent, inputs = lax.optimization_barrier((sent, inputs))
    partials = [partial] + [
        lax.ppermute(made, "z", ring(-k, nz)) for k, made in zip((2, 1, 3), sent)
    ]
    (own_in,) = in_hbm(jnp.concatenate(inputs, 0))
    (other_in,) = in_hbm(swap_cores(own_in))
    own_hidden, other_hidden = hidden_units(own_in, other_in, weights, unit_rows)
    heads = merge(after(place, own_hidden), partials)
    attention = [heads[0]] + [lax.ppermute(heads[k], "z", ring(k, nz)) for k in range(1, nz)]

    other_hidden, own_hidden = after((other_hidden, own_hidden), heads)
    own_part, other_part = down_units(own_hidden, other_hidden, weights, unit_rows)
    attention = after(tuple(attention), other_part, own_part)
    given = finish(other_part, attention, 1, weights, unit_rows, BF16)
    taken = [swap_cores(part) for part in given]
    kept = finish(after(own_part, *given), attention, 0, weights, unit_rows, F32)
    summed = stream.astype(F32) + kept[0] + taken[0].astype(F32)
    for k in (2, 1, 3):
        both = (kept[k] + taken[k].astype(F32)).astype(BF16)
        summed = summed + lax.ppermute(both, "z", ring(-k, nz)).astype(F32)
    return summed.astype(BF16)


def solution(mesh):
    names = ("y", "x", "z", "c")
    requests, others = mesh.devices.shape
    grid = Mesh(mesh.devices.reshape(requests, others // 8, 4, 2), names)
    rows = P(names, None)
    return jax.shard_map(
        on_device,
        mesh=grid,
        in_specs=(rows, rows, rows, rows, P(), P(), rows, rows, rows),
        out_specs=rows,
        check_vma=False,
    )
```

```python
import functools
import math

import jax
import jax.numpy as jnp
from jax import lax
from jax.experimental import pallas as pl
from jax.experimental.pallas import tpu as pltpu
from jax.sharding import Mesh, PartitionSpec as P

HD = 256
NORM_EPS = 1e-05
NEG = -(2.0**100)
LOG2E = 1.4426950408889634
SCORE = LOG2E / math.sqrt(HD)
MIB = 1 << 20
F32 = jnp.float32
BF16 = jnp.bfloat16


def ring(step, count):
    return [(i, (i + step) % count) for i in range(count)]


def swap_cores(value):
    return lax.ppermute(value, "c", [(0, 1), (1, 0)])


def params(mib):
    return pltpu.CompilerParams(vmem_limit_bytes=mib * MIB)


def dot(a, b, dims):
    return lax.dot_general(a, b, (dims, ((), ())), preferred_element_type=F32)


def pick_new(place, projections):
    rows, width = projections.shape
    heads = width // (2 * HD)

    def body(place_ref, source, own, other):
        c = place_ref[0]
        for j in range(heads):
            other[:, j * HD : (j + 1) * HD] = source[:, pl.ds((2 * j + 1 - c) * HD, HD)]
        for j in range(heads // 3):
            own[:, j * HD : (j + 1) * HD] = source[:, pl.ds((2 * j + c) * HD, HD)]

    return pl.pallas_call(
        body,
        grid_spec=pltpu.PrefetchScalarGridSpec(
            num_scalar_prefetch=1,
            grid=(1,),
            in_specs=[pl.BlockSpec((rows, width), lambda i, s: (0, 0))],
            out_specs=[
                pl.BlockSpec((rows, width // 6), lambda i, s: (0, 0)),
                pl.BlockSpec((rows, width // 2), lambda i, s: (0, 0)),
            ],
        ),
        out_shape=[
            jax.ShapeDtypeStruct((rows, width // 6), BF16),
            jax.ShapeDtypeStruct((rows, width // 2), BF16),
        ],
        compiler_params=params(16),
        name="pick_new",
    )(place, projections)


def pick_cache(place, keys, values):
    rows, width = keys.shape
    heads = width // (2 * HD)

    def body(place_ref, key_ref, value_ref, other, held, arrived, left):
        c = place_ref[0]
        copies = []
        for i, source in enumerate((key_ref, value_ref)):
            for j in range(heads):
                start = pl.multiple_of((2 * j + 1 - c) * HD, HD)
                columns = pl.ds(j * HD, HD)
                slot = held.at[i, :, columns]
                copies.append(
                    (
                        pltpu.make_async_copy(
                            source.at[:, pl.ds(start, HD)], slot, arrived.at[i * heads + j]
                        ),
                        pltpu.make_async_copy(
                            slot, other.at[i, :, columns], left.at[i * heads + j]
                        ),
                    )
                )
        for come, _ in copies:
            come.start()
        for come, leave in copies:
            come.wait()
            leave.start()
        for _, leave in copies:
            leave.wait()

    whole = pl.BlockSpec(memory_space=pl.ANY)
    return pl.pallas_call(
        body,
        grid_spec=pltpu.PrefetchScalarGridSpec(
            num_scalar_prefetch=1,
            grid=(1,),
            in_specs=[whole, whole],
            out_specs=pl.BlockSpec(memory_space=pltpu.HBM),
            scratch_shapes=[
                pltpu.VMEM((2, rows, width // 2), BF16),
                pltpu.SemaphoreType.DMA((2 * heads,)),
                pltpu.SemaphoreType.DMA((2 * heads,)),
            ],
        ),
        out_shape=jax.ShapeDtypeStruct((2, rows, width // 2), BF16),
        compiler_params=params(16),
        name="pick_cache",
    )(place, keys, values)


def norm_kernel(stream, gain, out):
    values = stream[...].astype(F32)
    width = values.shape[1]
    centred = values - jnp.sum(values, axis=-1, keepdims=True) * (1.0 / width)
    spread = jnp.sum(centred * centred, axis=-1, keepdims=True) * (1.0 / width)
    out[...] = (centred * lax.rsqrt(spread + NORM_EPS) * gain[...]).astype(BF16)


def layer_norm(stream, gain):
    return pl.pallas_call(
        norm_kernel,
        out_shape=jax.ShapeDtypeStruct(stream.shape, BF16),
        compiler_params=params(16),
        name="layer_norm",
    )(stream, gain.reshape(1, -1))


def attend_kernel(steps, place, ranges, *refs):
    blocks = len(steps)
    queries, refs = refs[:blocks], refs[blocks:]
    k0, k1, v0, v1, nk0, nk1, nv0, nv1 = refs[:8]
    outs, stats = refs[8 : 8 + blocks], refs[8 + blocks]
    j = pl.program_id(0)
    c, z, request = place[0], place[1], place[2]
    first, end = ranges[request, 0], ranges[request, 1]
    rows = queries[0].shape[0]
    half = rows // 2
    cache_rows = k0.shape[0]
    lane = lax.broadcasted_iota(jnp.int32, stats.shape[1:], 1)

    def bias(member):
        position = member * cache_rows + lax.broadcasted_iota(jnp.int32, (1, cache_rows), 1)
        return jnp.where((position >= first) & (position < end), 0.0, NEG).astype(F32)

    def order(shape, axis):
        place_in = lax.broadcasted_iota(jnp.int32, shape, axis)
        return jnp.where(place_in < half, place_in + c * half, place_in - c * half)

    bias_own, bias_other = bias(2 * z + c), bias(2 * z + 1 - c)
    new_keys = jnp.concatenate([nk0[...], nk1[...]], 0)
    new_values = jnp.concatenate([nv0[...], nv1[...]], 0)
    for i, (step, out) in enumerate(zip(steps, outs)):
        zq = lax.rem(z - step + 4, 4)
        query = queries[i][...]
        score_own = dot(query, k0[...], ((1,), (1,))) + bias_own
        score_other = dot(query, k1[...], ((1,), (1,))) + bias_other
        visible = z * rows + order((1, rows), 1) <= zq * rows + order((rows, 1), 0)
        score_new = jnp.where(visible, dot(query, new_keys, ((1,), (1,))), NEG)
        top = jnp.maximum(
            jnp.maximum(
                jnp.max(score_own, axis=-1, keepdims=True),
                jnp.max(score_other, axis=-1, keepdims=True),
            ),
            jnp.max(score_new, axis=-1, keepdims=True),
        )
        shift = top.astype(BF16).astype(F32)

        def weigh(score, values):
            weight = jnp.exp2((score - shift) * SCORE)
            return (
                jnp.sum(weight, axis=-1, keepdims=True),
                dot(weight.astype(BF16), values, ((1,), (0,))),
            )

        parts = [
            weigh(score_own, v0[...]),
            weigh(score_other, v1[...]),
            weigh(score_new, new_values),
        ]
        total = parts[0][0] + parts[1][0] + parts[2][0]
        out[:, pl.ds(pl.multiple_of(j * HD, HD), HD)] = (
            parts[0][1] + parts[1][1] + parts[2][1]
        ).astype(BF16)
        high = total.astype(BF16).astype(F32)
        kept = jnp.where(j == 0, 0.0, stats[i])
        kept = jnp.where(lane == 3 * j, shift, kept)
        kept = jnp.where(lane == 3 * j + 1, high, kept)
        kept = jnp.where(lane == 3 * j + 2, total - high, kept)
        stats[i] = kept
        out[:, out.shape[1] - 128 :] = kept.astype(BF16)


def attend(steps, place, ranges, queries, keys, values, projections, cache_in, new_in):
    rows, width = queries[0].shape
    blocks = len(steps)
    heads = width // HD
    cache_rows = keys.shape[0]
    new_rows = projections.shape[0]

    def columns(count, index):
        return pl.BlockSpec((count, HD), index)

    def received(i):
        return pl.BlockSpec((None, cache_rows, HD), lambda j, s, r: (i, 0, j))

    return pl.pallas_call(
        functools.partial(attend_kernel, steps),
        grid_spec=pltpu.PrefetchScalarGridSpec(
            num_scalar_prefetch=2,
            grid=(heads,),
            in_specs=[columns(rows, lambda j, s, r: (0, j))] * blocks
            + [
                columns(cache_rows, lambda j, s, r: (0, 2 * j + s[0])),
                received(0),
                columns(cache_rows, lambda j, s, r: (0, 2 * j + s[0])),
                received(1),
                columns(new_rows, lambda j, s, r: (0, 2 * heads + 2 * j + s[0])),
                columns(new_rows, lambda j, s, r: (0, heads + j)),
                columns(new_rows, lambda j, s, r: (0, 4 * heads + 2 * j + s[0])),
                columns(new_rows, lambda j, s, r: (0, 2 * heads + j)),
            ],
            out_specs=[pl.BlockSpec((rows, width + 128), lambda j, s, r: (0, 0))] * blocks,
            scratch_shapes=[pltpu.VMEM((blocks, rows, 128), F32)],
        ),
        out_shape=[jax.ShapeDtypeStruct((rows, width + 128), BF16)] * blocks,
        compiler_params=params(40),
        cost_estimate=pl.CostEstimate(
            flops=4 * blocks * rows * (2 * cache_rows + rows) * width,
            transcendentals=blocks * rows * (2 * cache_rows + rows) * heads,
            bytes_accessed=8 * cache_rows * width + 8 * blocks * rows * width,
        ),
        name="attend",
    )(
        place,
        ranges,
        *queries,
        keys,
        cache_in,
        values,
        cache_in,
        projections,
        new_in,
        projections,
        new_in,
    )


def merge_kernel(place, a, b, c, d, out):
    z = place[1]
    count = out.shape[0]
    parts = (a, b, c, d)
    base = a.shape[1] - 128
    stats = [part[:, base:].astype(F32) for part in parts]
    for j in range(count):
        shifts = [s[:, 3 * j : 3 * j + 1] for s in stats]
        totals = [s[:, 3 * j + 1 : 3 * j + 2] + s[:, 3 * j + 2 : 3 * j + 3] for s in stats]
        top = jnp.maximum(
            jnp.maximum(shifts[0], shifts[1]), jnp.maximum(shifts[2], shifts[3])
        )
        factors = [jnp.exp2((s - top) * SCORE) for s in shifts]
        total = sum(f * t for f, t in zip(factors, totals))
        summed = sum(
            f * part[:, j * HD : (j + 1) * HD].astype(F32) for f, part in zip(factors, parts)
        )
        out[lax.rem(j - z + count, count)] = (summed / total).astype(BF16)


def merge(place, parts):
    rows, width = parts[0].shape
    count = (width - 128) // HD
    whole = pl.BlockSpec((rows, width), lambda i, s: (0, 0))
    return pl.pallas_call(
        merge_kernel,
        grid_spec=pltpu.PrefetchScalarGridSpec(
            num_scalar_prefetch=1,
            grid=(1,),
            in_specs=[whole] * 4,
            out_specs=pl.BlockSpec((count, rows, HD), lambda i, s: (0, 0, 0)),
        ),
        out_shape=jax.ShapeDtypeStruct((count, rows, HD), BF16),
        compiler_params=params(12),
        name="merge",
    )(place, *parts)


def hidden_kernel(own_in, other_in, up_ref, own, other):
    shards, rows, width = up_ref.shape
    up = up_ref[...].reshape(shards * rows, width)
    for inputs, out in ((own_in, own), (other_in, other)):
        gates = dot(inputs[...], up, ((1,), (1,)))
        out[...] = (0.5 * gates * (1.0 + lax.erf(gates * math.sqrt(0.5)))).astype(BF16)


def hidden_units(own_in, other_in, weights, unit_rows):
    rows, width = own_in.shape
    shards = weights.shape[0]
    chunk = 4
    count = chunk * unit_rows
    whole = pl.BlockSpec((rows, width), lambda i: (0, 0))
    part = pl.BlockSpec((rows, count), lambda i: (0, i))
    return pl.pallas_call(
        hidden_kernel,
        grid=(shards // chunk,),
        in_specs=[
            whole,
            whole,
            pl.BlockSpec((chunk, unit_rows, width), lambda i: (i, 0, 0)),
        ],
        out_specs=[part, part],
        out_shape=[jax.ShapeDtypeStruct((rows, shards * unit_rows), BF16)] * 2,
        compiler_params=params(20),
        cost_estimate=pl.CostEstimate(
            flops=4 * rows * shards * unit_rows * width,
            transcendentals=0,
            bytes_accessed=2 * shards * unit_rows * width + 4 * rows * width,
        ),
        name="hidden_units",
    )(own_in, other_in, weights)


def down_kernel(own_hidden, other_hidden, down_ref, own, other):
    shards, rows, columns = down_ref.shape
    down = down_ref[...].reshape(shards * rows, columns)
    other[...] = dot(other_hidden[...], down, ((1,), (0,)))
    own[...] = dot(own_hidden[...], down, ((1,), (0,)))


def down_units(own_hidden, other_hidden, weights, unit_rows):
    rows, units = own_hidden.shape
    shards, _, width = weights.shape
    columns = 512
    whole = pl.BlockSpec((rows, units), lambda i: (0, 0))
    part = pl.BlockSpec((rows, columns), lambda i: (0, i))
    return pl.pallas_call(
        down_kernel,
        grid=(width // columns,),
        in_specs=[
            whole,
            whole,
            pl.BlockSpec((shards, unit_rows, columns), lambda i: (0, 1, i)),
        ],
        out_specs=[part, part],
        out_shape=[jax.ShapeDtypeStruct((rows, width), F32)] * 2,
        compiler_params=params(20),
        cost_estimate=pl.CostEstimate(
            flops=4 * rows * units * width,
            transcendentals=0,
            bytes_accessed=2 * units * width + 4 * rows * units + 8 * rows * width,
        ),
        name="down_units",
    )(own_hidden, other_hidden, weights)


def finish_kernel(partial, a0, a1, a2, a3, out_ref, *outs):
    shards, rows, columns = out_ref.shape
    heads = jnp.concatenate([a0[...], a1[...], a2[...], a3[...]], 0)
    out_rows = out_ref[...].reshape(shards * rows, columns)
    made = partial[...] + dot(heads, out_rows, ((1,), (0,)))
    count = made.shape[0] // len(outs)
    for i, out in enumerate(outs):
        out[...] = made[i * count : (i + 1) * count].astype(out.dtype)


def finish(partial, heads, side, weights, unit_rows, dtype):
    rows, width = partial.shape
    shards, shard_rows, _ = weights.shape
    out_rows = shard_rows - 2 * unit_rows
    count = rows // len(heads)
    columns = 512
    return pl.pallas_call(
        finish_kernel,
        grid=(width // columns,),
        in_specs=[pl.BlockSpec((rows, columns), lambda i: (0, i))]
        + [pl.BlockSpec((count, HD), lambda i: (side, 0))] * len(heads)
        + [
            pl.BlockSpec(
                (shards, out_rows, columns), lambda i: (0, 2 * unit_rows // out_rows, i)
            ),
        ],
        out_specs=[pl.BlockSpec((count, columns), lambda i: (0, i))] * len(heads),
        out_shape=[jax.ShapeDtypeStruct((count, width), dtype)] * len(heads),
        compiler_params=params(16),
        cost_estimate=pl.CostEstimate(
            flops=2 * rows * HD * width,
            transcendentals=0,
            bytes_accessed=2 * HD * width + 8 * rows * width,
        ),
        name="finish",
    )(partial, *heads, weights)


def head_owners(ny, nx, nz):
    pairs = []
    for y in range(ny):
        for x in range(nx):
            for z in range(nz):
                for c in range(2):
                    place = (x % 2) * 8 + z * 2 + c
                    target = ((place // nx * nx + place % nx) * nz + y) * 2 + x // 2
                    pairs.append((((y * nx + x) * nz + z) * 2 + c, target))
    return pairs


def in_hbm(*arrays):
    return tuple(pltpu.with_memory_space_constraint(array, pltpu.HBM) for array in arrays)


def after(value, *others):
    return lax.optimization_barrier((value, *others))[0]


def on_device(
    stream,
    projections,
    key_cache,
    value_cache,
    cache_range,
    norm_gain,
    out_weight,
    up_weight,
    down_weight,
):
    width = stream.shape[1]
    half = width // 2
    y, x, z, c = (lax.axis_index(name) for name in "yxzc")
    ny, nx, nz = (lax.axis_size(name) for name in "yxz")
    request = y * nx + x
    unit_rows = up_weight.shape[0]

    place = jnp.stack([c, z, request]).astype(jnp.int32)
    head_rows = lax.ppermute(out_weight, ("y", "x", "z", "c"), head_owners(ny, nx, nz))
    cached = in_hbm(key_cache, value_cache)
    own_query, new_out = pick_new(place, projections)
    new_in = swap_cores(new_out)
    cache_out = pick_cache(after(place, new_out), *cached)
    head_rows = after(head_rows, cache_out, new_in)
    weights = lax.all_gather(
        jnp.concatenate([up_weight, down_weight, head_rows], 0), ("y", "x"), axis=0
    )
    query = jnp.concatenate([own_query, new_in[:, :half]], 0)
    queries = [lax.ppermute(query, "z", ring(k, nz)) for k in (2, 1, 3)]
    cache_in = swap_cores(after(cache_out, query))
    context = (*cached, *in_hbm(projections), cache_in, new_in)
    (partial,) = attend((0,), place, cache_range, [query], *context)

    norm_gain, place_late = after((norm_gain, place), partial, *queries)
    normed = layer_norm(stream, norm_gain)
    place_late = after(place_late, normed)
    sent = attend((2, 1, 3), place_late, cache_range, queries, *context)
    inputs = [normed] + [lax.ppermute(normed, "z", ring(k, nz)) for k in range(1, nz)]
    inputs = after(inputs, *sent)
    partials = [partial] + [
        lax.ppermute(made, "z", ring(-k, nz)) for k, made in zip((2, 1, 3), sent)
    ]
    (own_in,) = in_hbm(jnp.concatenate(inputs, 0))
    (other_in,) = in_hbm(swap_cores(own_in))
    (weights,) = in_hbm(weights)
    own_hidden, other_hidden = hidden_units(own_in, other_in, weights, unit_rows)
    heads = merge(after(place, own_hidden), partials)
    attention = [heads[0]] + [lax.ppermute(heads[k], "z", ring(k, nz)) for k in range(1, nz)]

    other_hidden, own_hidden = after((other_hidden, own_hidden), heads)
    own_part, other_part = down_units(own_hidden, other_hidden, weights, unit_rows)
    attention = after(tuple(attention), other_part, own_part)
    given = finish(other_part, attention, 1, weights, unit_rows, BF16)
    taken = [swap_cores(part) for part in given]
    kept = finish(after(own_part, *given), attention, 0, weights, unit_rows, F32)
    summed = stream.astype(F32) + kept[0] + taken[0].astype(F32)
    for k in (2, 1, 3):
        both = (kept[k] + taken[k].astype(F32)).astype(BF16)
        summed = summed + lax.ppermute(both, "z", ring(-k, nz)).astype(F32)
    return summed.astype(BF16)


def solution(mesh):
    names = ("y", "x", "z", "c")
    requests, others = mesh.devices.shape
    grid = Mesh(mesh.devices.reshape(requests, others // 8, 4, 2), names)
    rows = P(names, None)
    return jax.shard_map(
        on_device,
        mesh=grid,
        in_specs=(rows, rows, rows, rows, P(), P(), rows, rows, rows),
        out_specs=rows,
        check_vma=False,
    )
```

```python
import functools
import math

import jax
import jax.numpy as jnp
from jax import lax
from jax.experimental import pallas as pl
from jax.experimental.pallas import tpu as pltpu
from jax.sharding import Mesh, PartitionSpec as P

HD = 256
NORM_EPS = 1e-05
NEG = -(2.0**100)
LOG2E = 1.4426950408889634
SCORE = LOG2E / math.sqrt(HD)
MIB = 1 << 20
F32 = jnp.float32
BF16 = jnp.bfloat16


def ring(step, count):
    return [(i, (i + step) % count) for i in range(count)]


def swap_cores(value):
    return lax.ppermute(value, "c", [(0, 1), (1, 0)])


def params(mib):
    return pltpu.CompilerParams(vmem_limit_bytes=mib * MIB)


def dot(a, b, dims):
    return lax.dot_general(a, b, (dims, ((), ())), preferred_element_type=F32)


def pick_new(place, projections):
    rows, width = projections.shape
    heads = width // (2 * HD)

    def body(place_ref, source, own, other):
        c = place_ref[0]
        for j in range(heads):
            other[:, j * HD : (j + 1) * HD] = source[:, pl.ds((2 * j + 1 - c) * HD, HD)]
        for j in range(heads // 3):
            own[:, j * HD : (j + 1) * HD] = source[:, pl.ds((2 * j + c) * HD, HD)]

    return pl.pallas_call(
        body,
        grid_spec=pltpu.PrefetchScalarGridSpec(
            num_scalar_prefetch=1,
            grid=(1,),
            in_specs=[pl.BlockSpec((rows, width), lambda i, s: (0, 0))],
            out_specs=[
                pl.BlockSpec((rows, width // 6), lambda i, s: (0, 0)),
                pl.BlockSpec((rows, width // 2), lambda i, s: (0, 0)),
            ],
        ),
        out_shape=[
            jax.ShapeDtypeStruct((rows, width // 6), BF16),
            jax.ShapeDtypeStruct((rows, width // 2), BF16),
        ],
        compiler_params=params(16),
        name="pick_new",
    )(place, projections)


def pick_cache(place, keys, values):
    rows, width = keys.shape
    heads = width // (2 * HD)

    def body(place_ref, key_ref, value_ref, other, held, arrived, left):
        c = place_ref[0]
        copies = []
        for i, source in enumerate((key_ref, value_ref)):
            for j in range(heads):
                start = pl.multiple_of((2 * j + 1 - c) * HD, HD)
                columns = pl.ds(j * HD, HD)
                slot = held.at[i, :, columns]
                copies.append(
                    (
                        pltpu.make_async_copy(
                            source.at[:, pl.ds(start, HD)], slot, arrived.at[i * heads + j]
                        ),
                        pltpu.make_async_copy(
                            slot, other.at[i, :, columns], left.at[i * heads + j]
                        ),
                    )
                )
        for come, _ in copies:
            come.start()
        for come, leave in copies:
            come.wait()
            leave.start()
        for _, leave in copies:
            leave.wait()

    whole = pl.BlockSpec(memory_space=pl.ANY)
    return pl.pallas_call(
        body,
        grid_spec=pltpu.PrefetchScalarGridSpec(
            num_scalar_prefetch=1,
            grid=(1,),
            in_specs=[whole, whole],
            out_specs=pl.BlockSpec(memory_space=pltpu.HBM),
            scratch_shapes=[
                pltpu.VMEM((2, rows, width // 2), BF16),
                pltpu.SemaphoreType.DMA((2 * heads,)),
                pltpu.SemaphoreType.DMA((2 * heads,)),
            ],
        ),
        out_shape=pltpu.HBM((2, rows, width // 2), BF16),
        compiler_params=params(16),
        name="pick_cache",
    )(place, keys, values)


def norm_kernel(stream, gain, out):
    values = stream[...].astype(F32)
    width = values.shape[1]
    centred = values - jnp.sum(values, axis=-1, keepdims=True) * (1.0 / width)
    spread = jnp.sum(centred * centred, axis=-1, keepdims=True) * (1.0 / width)
    out[...] = (centred * lax.rsqrt(spread + NORM_EPS) * gain[...]).astype(BF16)


def layer_norm(stream, gain):
    return pl.pallas_call(
        norm_kernel,
        out_shape=jax.ShapeDtypeStruct(stream.shape, BF16),
        compiler_params=params(16),
        name="layer_norm",
    )(stream, gain.reshape(1, -1))


def attend_kernel(steps, place, ranges, *refs):
    blocks = len(steps)
    queries, refs = refs[:blocks], refs[blocks:]
    k0, k1, v0, v1, nk0, nk1, nv0, nv1 = refs[:8]
    outs, stats = refs[8 : 8 + blocks], refs[8 + blocks]
    j = pl.program_id(0)
    c, z, request = place[0], place[1], place[2]
    first, end = ranges[request, 0], ranges[request, 1]
    rows = queries[0].shape[0]
    half = rows // 2
    cache_rows = k0.shape[0]
    lane = lax.broadcasted_iota(jnp.int32, stats.shape[1:], 1)

    def bias(member):
        position = member * cache_rows + lax.broadcasted_iota(jnp.int32, (1, cache_rows), 1)
        return jnp.where((position >= first) & (position < end), 0.0, NEG).astype(F32)

    def order(shape, axis):
        place_in = lax.broadcasted_iota(jnp.int32, shape, axis)
        return jnp.where(place_in < half, place_in + c * half, place_in - c * half)

    bias_own, bias_other = bias(2 * z + c), bias(2 * z + 1 - c)
    new_keys = jnp.concatenate([nk0[...], nk1[...]], 0)
    new_values = jnp.concatenate([nv0[...], nv1[...]], 0)
    for i, (step, out) in enumerate(zip(steps, outs)):
        zq = lax.rem(z - step + 4, 4)
        query = queries[i][...]
        score_own = dot(query, k0[...], ((1,), (1,))) + bias_own
        score_other = dot(query, k1[...], ((1,), (1,))) + bias_other
        visible = z * rows + order((1, rows), 1) <= zq * rows + order((rows, 1), 0)
        score_new = jnp.where(visible, dot(query, new_keys, ((1,), (1,))), NEG)
        top = jnp.maximum(
            jnp.maximum(
                jnp.max(score_own, axis=-1, keepdims=True),
                jnp.max(score_other, axis=-1, keepdims=True),
            ),
            jnp.max(score_new, axis=-1, keepdims=True),
        )
        shift = top.astype(BF16).astype(F32)

        def weigh(score, values):
            weight = jnp.exp2((score - shift) * SCORE)
            return (
                jnp.sum(weight, axis=-1, keepdims=True),
                dot(weight.astype(BF16), values, ((1,), (0,))),
            )

        parts = [
            weigh(score_own, v0[...]),
            weigh(score_other, v1[...]),
            weigh(score_new, new_values),
        ]
        total = parts[0][0] + parts[1][0] + parts[2][0]
        out[:, pl.ds(pl.multiple_of(j * HD, HD), HD)] = (
            parts[0][1] + parts[1][1] + parts[2][1]
        ).astype(BF16)
        high = total.astype(BF16).astype(F32)
        kept = jnp.where(j == 0, 0.0, stats[i])
        kept = jnp.where(lane == 3 * j, shift, kept)
        kept = jnp.where(lane == 3 * j + 1, high, kept)
        kept = jnp.where(lane == 3 * j + 2, total - high, kept)
        stats[i] = kept
        out[:, out.shape[1] - 128 :] = kept.astype(BF16)


def attend(steps, place, ranges, queries, keys, values, projections, cache_in, new_in):
    rows, width = queries[0].shape
    blocks = len(steps)
    heads = width // HD
    cache_rows = keys.shape[0]
    new_rows = projections.shape[0]

    def columns(count, index):
        return pl.BlockSpec((count, HD), index)

    def received(i):
        return pl.BlockSpec((None, cache_rows, HD), lambda j, s, r: (i, 0, j))

    return pl.pallas_call(
        functools.partial(attend_kernel, steps),
        grid_spec=pltpu.PrefetchScalarGridSpec(
            num_scalar_prefetch=2,
            grid=(heads,),
            in_specs=[columns(rows, lambda j, s, r: (0, j))] * blocks
            + [
                columns(cache_rows, lambda j, s, r: (0, 2 * j + s[0])),
                received(0),
                columns(cache_rows, lambda j, s, r: (0, 2 * j + s[0])),
                received(1),
                columns(new_rows, lambda j, s, r: (0, 2 * heads + 2 * j + s[0])),
                columns(new_rows, lambda j, s, r: (0, heads + j)),
                columns(new_rows, lambda j, s, r: (0, 4 * heads + 2 * j + s[0])),
                columns(new_rows, lambda j, s, r: (0, 2 * heads + j)),
            ],
            out_specs=[pl.BlockSpec((rows, width + 128), lambda j, s, r: (0, 0))] * blocks,
            scratch_shapes=[pltpu.VMEM((blocks, rows, 128), F32)],
        ),
        out_shape=[jax.ShapeDtypeStruct((rows, width + 128), BF16)] * blocks,
        compiler_params=params(40),
        cost_estimate=pl.CostEstimate(
            flops=4 * blocks * rows * (2 * cache_rows + rows) * width,
            transcendentals=blocks * rows * (2 * cache_rows + rows) * heads,
            bytes_accessed=8 * cache_rows * width + 8 * blocks * rows * width,
        ),
        name="attend",
    )(
        place,
        ranges,
        *queries,
        keys,
        cache_in,
        values,
        cache_in,
        projections,
        new_in,
        projections,
        new_in,
    )


def merge_kernel(place, a, b, c, d, out):
    z = place[1]
    count = out.shape[0]
    parts = (a, b, c, d)
    base = a.shape[1] - 128
    stats = [part[:, base:].astype(F32) for part in parts]
    for j in range(count):
        shifts = [s[:, 3 * j : 3 * j + 1] for s in stats]
        totals = [s[:, 3 * j + 1 : 3 * j + 2] + s[:, 3 * j + 2 : 3 * j + 3] for s in stats]
        top = jnp.maximum(
            jnp.maximum(shifts[0], shifts[1]), jnp.maximum(shifts[2], shifts[3])
        )
        factors = [jnp.exp2((s - top) * SCORE) for s in shifts]
        total = sum(f * t for f, t in zip(factors, totals))
        summed = sum(
            f * part[:, j * HD : (j + 1) * HD].astype(F32) for f, part in zip(factors, parts)
        )
        out[lax.rem(j - z + count, count)] = (summed / total).astype(BF16)


def merge(place, parts):
    rows, width = parts[0].shape
    count = (width - 128) // HD
    whole = pl.BlockSpec((rows, width), lambda i, s: (0, 0))
    return pl.pallas_call(
        merge_kernel,
        grid_spec=pltpu.PrefetchScalarGridSpec(
            num_scalar_prefetch=1,
            grid=(1,),
            in_specs=[whole] * 4,
            out_specs=pl.BlockSpec((count, rows, HD), lambda i, s: (0, 0, 0)),
        ),
        out_shape=jax.ShapeDtypeStruct((count, rows, HD), BF16),
        compiler_params=params(12),
        name="merge",
    )(place, *parts)


def hidden_kernel(own_in, other_in, up_ref, own, other):
    shards, rows, width = up_ref.shape
    up = up_ref[...].reshape(shards * rows, width)
    for inputs, out in ((own_in, own), (other_in, other)):
        gates = dot(inputs[...], up, ((1,), (1,)))
        out[...] = (0.5 * gates * (1.0 + lax.erf(gates * math.sqrt(0.5)))).astype(BF16)


def hidden_units(own_in, other_in, weights, unit_rows):
    rows, width = own_in.shape
    shards = weights.shape[0]
    chunk = 4
    count = chunk * unit_rows
    whole = pl.BlockSpec((rows, width), lambda i: (0, 0))
    part = pl.BlockSpec((rows, count), lambda i: (0, i))
    return pl.pallas_call(
        hidden_kernel,
        grid=(shards // chunk,),
        in_specs=[
            whole,
            whole,
            pl.BlockSpec((chunk, unit_rows, width), lambda i: (i, 0, 0)),
        ],
        out_specs=[part, part],
        out_shape=[jax.ShapeDtypeStruct((rows, shards * unit_rows), BF16)] * 2,
        compiler_params=params(20),
        cost_estimate=pl.CostEstimate(
            flops=4 * rows * shards * unit_rows * width,
            transcendentals=0,
            bytes_accessed=2 * shards * unit_rows * width + 4 * rows * width,
        ),
        name="hidden_units",
    )(own_in, other_in, weights)


def down_kernel(own_hidden, other_hidden, down_ref, own, other):
    shards, rows, columns = down_ref.shape
    down = down_ref[...].reshape(shards * rows, columns)
    other[...] = dot(other_hidden[...], down, ((1,), (0,)))
    own[...] = dot(own_hidden[...], down, ((1,), (0,)))


def down_units(own_hidden, other_hidden, weights, unit_rows):
    rows, units = own_hidden.shape
    shards, _, width = weights.shape
    columns = 512
    whole = pl.BlockSpec((rows, units), lambda i: (0, 0))
    part = pl.BlockSpec((rows, columns), lambda i: (0, i))
    return pl.pallas_call(
        down_kernel,
        grid=(width // columns,),
        in_specs=[
            whole,
            whole,
            pl.BlockSpec((shards, unit_rows, columns), lambda i: (0, 1, i)),
        ],
        out_specs=[part, part],
        out_shape=[jax.ShapeDtypeStruct((rows, width), F32)] * 2,
        compiler_params=params(20),
        cost_estimate=pl.CostEstimate(
            flops=4 * rows * units * width,
            transcendentals=0,
            bytes_accessed=2 * units * width + 4 * rows * units + 8 * rows * width,
        ),
        name="down_units",
    )(own_hidden, other_hidden, weights)


def finish_kernel(partial, a0, a1, a2, a3, out_ref, *outs):
    shards, rows, columns = out_ref.shape
    heads = jnp.concatenate([a0[...], a1[...], a2[...], a3[...]], 0)
    out_rows = out_ref[...].reshape(shards * rows, columns)
    made = partial[...] + dot(heads, out_rows, ((1,), (0,)))
    count = made.shape[0] // len(outs)
    for i, out in enumerate(outs):
        out[...] = made[i * count : (i + 1) * count].astype(out.dtype)


def finish(partial, heads, side, weights, unit_rows, dtype):
    rows, width = partial.shape
    shards, shard_rows, _ = weights.shape
    out_rows = shard_rows - 2 * unit_rows
    count = rows // len(heads)
    columns = 512
    return pl.pallas_call(
        finish_kernel,
        grid=(width // columns,),
        in_specs=[pl.BlockSpec((rows, columns), lambda i: (0, i))]
        + [pl.BlockSpec((count, HD), lambda i: (side, 0))] * len(heads)
        + [
            pl.BlockSpec(
                (shards, out_rows, columns), lambda i: (0, 2 * unit_rows // out_rows, i)
            ),
        ],
        out_specs=[pl.BlockSpec((count, columns), lambda i: (0, i))] * len(heads),
        out_shape=[jax.ShapeDtypeStruct((count, width), dtype)] * len(heads),
        compiler_params=params(16),
        cost_estimate=pl.CostEstimate(
            flops=2 * rows * HD * width,
            transcendentals=0,
            bytes_accessed=2 * HD * width + 8 * rows * width,
        ),
        name="finish",
    )(partial, *heads, weights)


def head_owners(ny, nx, nz):
    pairs = []
    for y in range(ny):
        for x in range(nx):
            for z in range(nz):
                for c in range(2):
                    place = (x % 2) * 8 + z * 2 + c
                    target = ((place // nx * nx + place % nx) * nz + y) * 2 + x // 2
                    pairs.append((((y * nx + x) * nz + z) * 2 + c, target))
    return pairs


def in_hbm(*arrays):
    return tuple(pltpu.with_memory_space_constraint(array, pltpu.HBM) for array in arrays)


def after(value, *others):
    return lax.optimization_barrier((value, *others))[0]


def on_device(
    stream,
    projections,
    key_cache,
    value_cache,
    cache_range,
    norm_gain,
    out_weight,
    up_weight,
    down_weight,
):
    width = stream.shape[1]
    half = width // 2
    y, x, z, c = (lax.axis_index(name) for name in "yxzc")
    ny, nx, nz = (lax.axis_size(name) for name in "yxz")
    request = y * nx + x
    unit_rows = up_weight.shape[0]

    place = jnp.stack([c, z, request]).astype(jnp.int32)
    head_rows = lax.ppermute(out_weight, ("y", "x", "z", "c"), head_owners(ny, nx, nz))
    cached = in_hbm(key_cache, value_cache)
    own_query, new_out = pick_new(place, projections)
    new_in = swap_cores(new_out)
    cache_out = pick_cache(after(place, new_out), *cached)
    head_rows = after(head_rows, cache_out)
    weights = lax.all_gather(
        jnp.concatenate([up_weight, down_weight, head_rows], 0), ("y", "x"), axis=0
    )
    (query,) = in_hbm(jnp.concatenate([own_query, new_in[:, :half]], 0))
    queries = [lax.ppermute(query, "z", ring(k, nz)) for k in (2, 1, 3)]
    cache_in = swap_cores(after(cache_out, query))
    context = (*cached, *in_hbm(projections), cache_in, new_in)
    norm_gain, place_late = after((norm_gain, place), *queries, cache_in)
    normed = layer_norm(stream, norm_gain)
    place_late = after(place_late, normed)
    partial, *sent = attend((0, 2, 1, 3), place_late, cache_range, [query, *queries], *context)
    inputs = [normed] + [lax.ppermute(normed, "z", ring(k, nz)) for k in range(1, nz)]
    sent, inputs = lax.optimization_barrier((sent, inputs))
    partials = [partial] + [
        lax.ppermute(made, "z", ring(-k, nz)) for k, made in zip((2, 1, 3), sent)
    ]
    (own_in,) = in_hbm(jnp.concatenate(inputs, 0))
    (other_in,) = in_hbm(swap_cores(own_in))
    own_hidden, other_hidden = hidden_units(own_in, other_in, *in_hbm(weights), unit_rows)
    heads = merge(after(place, own_hidden), partials)
    attention = [heads[0]] + [lax.ppermute(heads[k], "z", ring(k, nz)) for k in range(1, nz)]

    other_hidden, own_hidden = after((other_hidden, own_hidden), heads)
    own_part, other_part = down_units(own_hidden, other_hidden, weights, unit_rows)
    attention = after(tuple(attention), other_part, own_part)
    given = finish(other_part, attention, 1, weights, unit_rows, BF16)
    taken = [swap_cores(part) for part in given]
    kept = finish(after(own_part, *given), attention, 0, weights, unit_rows, F32)
    summed = stream.astype(F32) + kept[0] + taken[0].astype(F32)
    for k in (2, 1, 3):
        both = (kept[k] + taken[k].astype(F32)).astype(BF16)
        summed = summed + lax.ppermute(both, "z", ring(-k, nz)).astype(F32)
    return summed.astype(BF16)


def solution(mesh):
    names = ("y", "x", "z", "c")
    requests, others = mesh.devices.shape
    grid = Mesh(mesh.devices.reshape(requests, others // 8, 4, 2), names)
    rows = P(names, None)
    return jax.shard_map(
        on_device,
        mesh=grid,
        in_specs=(rows, rows, rows, rows, P(), P(), rows, rows, rows),
        out_specs=rows,
        check_vma=False,
    )
```

```python
import functools
import math

import jax
import jax.numpy as jnp
from jax import lax
from jax.experimental import pallas as pl
from jax.experimental.pallas import tpu as pltpu
from jax.sharding import Mesh, PartitionSpec as P

HD = 256
NORM_EPS = 1e-05
NEG = -(2.0**100)
LOG2E = 1.4426950408889634
SCORE = LOG2E / math.sqrt(HD)
MIB = 1 << 20
F32 = jnp.float32
BF16 = jnp.bfloat16


def ring(step, count):
    return [(i, (i + step) % count) for i in range(count)]


def swap_cores(value):
    return lax.ppermute(value, "c", [(0, 1), (1, 0)])


def params(mib):
    return pltpu.CompilerParams(vmem_limit_bytes=mib * MIB)


def dot(a, b, dims):
    return lax.dot_general(a, b, (dims, ((), ())), preferred_element_type=F32)


def pick_new(place, projections):
    rows, width = projections.shape
    heads = width // (2 * HD)

    def body(place_ref, source, own, other):
        c = place_ref[0]
        for j in range(heads):
            other[:, j * HD : (j + 1) * HD] = source[:, pl.ds((2 * j + 1 - c) * HD, HD)]
        for j in range(heads // 3):
            own[:, j * HD : (j + 1) * HD] = source[:, pl.ds((2 * j + c) * HD, HD)]

    return pl.pallas_call(
        body,
        grid_spec=pltpu.PrefetchScalarGridSpec(
            num_scalar_prefetch=1,
            grid=(1,),
            in_specs=[pl.BlockSpec((rows, width), lambda i, s: (0, 0))],
            out_specs=[
                pl.BlockSpec((rows, width // 6), lambda i, s: (0, 0)),
                pl.BlockSpec((rows, width // 2), lambda i, s: (0, 0)),
            ],
        ),
        out_shape=[
            jax.ShapeDtypeStruct((rows, width // 6), BF16),
            jax.ShapeDtypeStruct((rows, width // 2), BF16),
        ],
        compiler_params=params(16),
        name="pick_new",
    )(place, projections)


def pick_cache(place, keys, values):
    rows, width = keys.shape
    heads = width // (2 * HD)

    def body(place_ref, key_ref, value_ref, other, held, arrived, left):
        c = place_ref[0]
        copies = []
        for i, source in enumerate((key_ref, value_ref)):
            for j in range(heads):
                start = pl.multiple_of((2 * j + 1 - c) * HD, HD)
                columns = pl.ds(j * HD, HD)
                slot = held.at[i, :, columns]
                copies.append(
                    (
                        pltpu.make_async_copy(
                            source.at[:, pl.ds(start, HD)], slot, arrived.at[i * heads + j]
                        ),
                        pltpu.make_async_copy(
                            slot, other.at[i, :, columns], left.at[i * heads + j]
                        ),
                    )
                )
        ahead = 3
        for come, _ in copies[:ahead]:
            come.start()
        for i, (come, leave) in enumerate(copies):
            come.wait()
            leave.start()
            if i + ahead < len(copies):
                copies[i + ahead][0].start()
        for _, leave in copies:
            leave.wait()

    whole = pl.BlockSpec(memory_space=pl.ANY)
    return pl.pallas_call(
        body,
        grid_spec=pltpu.PrefetchScalarGridSpec(
            num_scalar_prefetch=1,
            grid=(1,),
            in_specs=[whole, whole],
            out_specs=pl.BlockSpec(memory_space=pltpu.HBM),
            scratch_shapes=[
                pltpu.VMEM((2, rows, width // 2), BF16),
                pltpu.SemaphoreType.DMA((2 * heads,)),
                pltpu.SemaphoreType.DMA((2 * heads,)),
            ],
        ),
        out_shape=pltpu.HBM((2, rows, width // 2), BF16),
        compiler_params=params(16),
        name="pick_cache",
    )(place, keys, values)


def norm_kernel(stream, gain, out):
    values = stream[...].astype(F32)
    width = values.shape[1]
    centred = values - jnp.sum(values, axis=-1, keepdims=True) * (1.0 / width)
    spread = jnp.sum(centred * centred, axis=-1, keepdims=True) * (1.0 / width)
    out[...] = (centred * lax.rsqrt(spread + NORM_EPS) * gain[...]).astype(BF16)


def layer_norm(stream, gain):
    return pl.pallas_call(
        norm_kernel,
        out_shape=jax.ShapeDtypeStruct(stream.shape, BF16),
        compiler_params=params(16),
        name="layer_norm",
    )(stream, gain.reshape(1, -1))


def attend_kernel(steps, place, ranges, *refs):
    blocks = len(steps)
    queries, refs = refs[:blocks], refs[blocks:]
    k0, k1, v0, v1, nk0, nk1, nv0, nv1 = refs[:8]
    outs, stats = refs[8 : 8 + blocks], refs[8 + blocks]
    j = pl.program_id(0)
    c, z, request = place[0], place[1], place[2]
    first, end = ranges[request, 0], ranges[request, 1]
    rows = queries[0].shape[0]
    half = rows // 2
    cache_rows = k0.shape[0]
    lane = lax.broadcasted_iota(jnp.int32, stats.shape[1:], 1)

    def bias(member):
        position = member * cache_rows + lax.broadcasted_iota(jnp.int32, (1, cache_rows), 1)
        return jnp.where((position >= first) & (position < end), 0.0, NEG).astype(F32)

    def order(shape, axis):
        place_in = lax.broadcasted_iota(jnp.int32, shape, axis)
        return jnp.where(place_in < half, place_in + c * half, place_in - c * half)

    bias_own, bias_other = bias(2 * z + c), bias(2 * z + 1 - c)
    new_keys = jnp.concatenate([nk0[...], nk1[...]], 0)
    new_values = jnp.concatenate([nv0[...], nv1[...]], 0)
    for i, (step, out) in enumerate(zip(steps, outs)):
        zq = lax.rem(z - step + 4, 4)
        query = queries[i][...]
        score_own = dot(query, k0[...], ((1,), (1,))) + bias_own
        score_other = dot(query, k1[...], ((1,), (1,))) + bias_other
        visible = z * rows + order((1, rows), 1) <= zq * rows + order((rows, 1), 0)
        score_new = jnp.where(visible, dot(query, new_keys, ((1,), (1,))), NEG)
        top = jnp.maximum(
            jnp.maximum(
                jnp.max(score_own, axis=-1, keepdims=True),
                jnp.max(score_other, axis=-1, keepdims=True),
            ),
            jnp.max(score_new, axis=-1, keepdims=True),
        )
        shift = top.astype(BF16).astype(F32)

        def weigh(score, values):
            weight = jnp.exp2((score - shift) * SCORE)
            return (
                jnp.sum(weight, axis=-1, keepdims=True),
                dot(weight.astype(BF16), values, ((1,), (0,))),
            )

        parts = [
            weigh(score_own, v0[...]),
            weigh(score_other, v1[...]),
            weigh(score_new, new_values),
        ]
        total = parts[0][0] + parts[1][0] + parts[2][0]
        out[:, pl.ds(pl.multiple_of(j * HD, HD), HD)] = (
            parts[0][1] + parts[1][1] + parts[2][1]
        ).astype(BF16)
        high = total.astype(BF16).astype(F32)
        kept = jnp.where(j == 0, 0.0, stats[i])
        kept = jnp.where(lane == 3 * j, shift, kept)
        kept = jnp.where(lane == 3 * j + 1, high, kept)
        kept = jnp.where(lane == 3 * j + 2, total - high, kept)
        stats[i] = kept
        out[:, out.shape[1] - 128 :] = kept.astype(BF16)


def attend(steps, place, ranges, queries, keys, values, projections, cache_in, new_in):
    rows, width = queries[0].shape
    blocks = len(steps)
    heads = width // HD
    cache_rows = keys.shape[0]
    new_rows = projections.shape[0]

    def columns(count, index):
        return pl.BlockSpec((count, HD), index)

    def received(i):
        return pl.BlockSpec((None, cache_rows, HD), lambda j, s, r: (i, 0, j))

    return pl.pallas_call(
        functools.partial(attend_kernel, steps),
        grid_spec=pltpu.PrefetchScalarGridSpec(
            num_scalar_prefetch=2,
            grid=(heads,),
            in_specs=[columns(rows, lambda j, s, r: (0, j))] * blocks
            + [
                columns(cache_rows, lambda j, s, r: (0, 2 * j + s[0])),
                received(0),
                columns(cache_rows, lambda j, s, r: (0, 2 * j + s[0])),
                received(1),
                columns(new_rows, lambda j, s, r: (0, 2 * heads + 2 * j + s[0])),
                columns(new_rows, lambda j, s, r: (0, heads + j)),
                columns(new_rows, lambda j, s, r: (0, 4 * heads + 2 * j + s[0])),
                columns(new_rows, lambda j, s, r: (0, 2 * heads + j)),
            ],
            out_specs=[pl.BlockSpec((rows, width + 128), lambda j, s, r: (0, 0))] * blocks,
            scratch_shapes=[pltpu.VMEM((blocks, rows, 128), F32)],
        ),
        out_shape=[jax.ShapeDtypeStruct((rows, width + 128), BF16)] * blocks,
        compiler_params=params(40),
        cost_estimate=pl.CostEstimate(
            flops=4 * blocks * rows * (2 * cache_rows + rows) * width,
            transcendentals=blocks * rows * (2 * cache_rows + rows) * heads,
            bytes_accessed=8 * cache_rows * width + 8 * blocks * rows * width,
        ),
        name="attend",
    )(
        place,
        ranges,
        *queries,
        keys,
        cache_in,
        values,
        cache_in,
        projections,
        new_in,
        projections,
        new_in,
    )


def merge_kernel(place, a, b, c, d, out):
    z = place[1]
    count = out.shape[0]
    parts = (a, b, c, d)
    base = a.shape[1] - 128
    stats = [part[:, base:].astype(F32) for part in parts]
    for j in range(count):
        shifts = [s[:, 3 * j : 3 * j + 1] for s in stats]
        totals = [s[:, 3 * j + 1 : 3 * j + 2] + s[:, 3 * j + 2 : 3 * j + 3] for s in stats]
        top = jnp.maximum(
            jnp.maximum(shifts[0], shifts[1]), jnp.maximum(shifts[2], shifts[3])
        )
        factors = [jnp.exp2((s - top) * SCORE) for s in shifts]
        total = sum(f * t for f, t in zip(factors, totals))
        summed = sum(
            f * part[:, j * HD : (j + 1) * HD].astype(F32) for f, part in zip(factors, parts)
        )
        out[lax.rem(j - z + count, count)] = (summed / total).astype(BF16)


def merge(place, parts):
    rows, width = parts[0].shape
    count = (width - 128) // HD
    whole = pl.BlockSpec((rows, width), lambda i, s: (0, 0))
    return pl.pallas_call(
        merge_kernel,
        grid_spec=pltpu.PrefetchScalarGridSpec(
            num_scalar_prefetch=1,
            grid=(1,),
            in_specs=[whole] * 4,
            out_specs=pl.BlockSpec((count, rows, HD), lambda i, s: (0, 0, 0)),
        ),
        out_shape=jax.ShapeDtypeStruct((count, rows, HD), BF16),
        compiler_params=params(12),
        name="merge",
    )(place, *parts)


def hidden_kernel(own_in, other_in, up_ref, own, other):
    shards, rows, width = up_ref.shape
    up = up_ref[...].reshape(shards * rows, width)
    for inputs, out in ((own_in, own), (other_in, other)):
        gates = dot(inputs[...], up, ((1,), (1,)))
        out[...] = (0.5 * gates * (1.0 + lax.erf(gates * math.sqrt(0.5)))).astype(BF16)


def hidden_units(own_in, other_in, weights, unit_rows):
    rows, width = own_in.shape
    shards = weights.shape[0]
    chunk = 4
    count = chunk * unit_rows
    whole = pl.BlockSpec((rows, width), lambda i: (0, 0))
    part = pl.BlockSpec((rows, count), lambda i: (0, i))
    return pl.pallas_call(
        hidden_kernel,
        grid=(shards // chunk,),
        in_specs=[
            whole,
            whole,
            pl.BlockSpec((chunk, unit_rows, width), lambda i: (i, 0, 0)),
        ],
        out_specs=[part, part],
        out_shape=[jax.ShapeDtypeStruct((rows, shards * unit_rows), BF16)] * 2,
        compiler_params=params(20),
        cost_estimate=pl.CostEstimate(
            flops=4 * rows * shards * unit_rows * width,
            transcendentals=0,
            bytes_accessed=2 * shards * unit_rows * width + 4 * rows * width,
        ),
        name="hidden_units",
    )(own_in, other_in, weights)


def down_kernel(own_hidden, other_hidden, down_ref, own, other):
    shards, rows, columns = down_ref.shape
    down = down_ref[...].reshape(shards * rows, columns)
    other[...] = dot(other_hidden[...], down, ((1,), (0,)))
    own[...] = dot(own_hidden[...], down, ((1,), (0,)))


def down_units(own_hidden, other_hidden, weights, unit_rows):
    rows, units = own_hidden.shape
    shards, _, width = weights.shape
    columns = 512
    whole = pl.BlockSpec((rows, units), lambda i: (0, 0))
    part = pl.BlockSpec((rows, columns), lambda i: (0, i))
    return pl.pallas_call(
        down_kernel,
        grid=(width // columns,),
        in_specs=[
            whole,
            whole,
            pl.BlockSpec((shards, unit_rows, columns), lambda i: (0, 1, i)),
        ],
        out_specs=[part, part],
        out_shape=[jax.ShapeDtypeStruct((rows, width), F32)] * 2,
        compiler_params=params(20),
        cost_estimate=pl.CostEstimate(
            flops=4 * rows * units * width,
            transcendentals=0,
            bytes_accessed=2 * units * width + 4 * rows * units + 8 * rows * width,
        ),
        name="down_units",
    )(own_hidden, other_hidden, weights)


def finish_kernel(partial, a0, a1, a2, a3, out_ref, *outs):
    shards, rows, columns = out_ref.shape
    heads = jnp.concatenate([a0[...], a1[...], a2[...], a3[...]], 0)
    out_rows = out_ref[...].reshape(shards * rows, columns)
    made = partial[...] + dot(heads, out_rows, ((1,), (0,)))
    count = made.shape[0] // len(outs)
    for i, out in enumerate(outs):
        out[...] = made[i * count : (i + 1) * count].astype(out.dtype)


def finish(partial, heads, side, weights, unit_rows, dtype):
    rows, width = partial.shape
    shards, shard_rows, _ = weights.shape
    out_rows = shard_rows - 2 * unit_rows
    count = rows // len(heads)
    columns = 512
    return pl.pallas_call(
        finish_kernel,
        grid=(width // columns,),
        in_specs=[pl.BlockSpec((rows, columns), lambda i: (0, i))]
        + [pl.BlockSpec((count, HD), lambda i: (side, 0))] * len(heads)
        + [
            pl.BlockSpec(
                (shards, out_rows, columns), lambda i: (0, 2 * unit_rows // out_rows, i)
            ),
        ],
        out_specs=[pl.BlockSpec((count, columns), lambda i: (0, i))] * len(heads),
        out_shape=[jax.ShapeDtypeStruct((count, width), dtype)] * len(heads),
        compiler_params=params(16),
        cost_estimate=pl.CostEstimate(
            flops=2 * rows * HD * width,
            transcendentals=0,
            bytes_accessed=2 * HD * width + 8 * rows * width,
        ),
        name="finish",
    )(partial, *heads, weights)


def head_owners(ny, nx, nz):
    pairs = []
    for y in range(ny):
        for x in range(nx):
            for z in range(nz):
                for c in range(2):
                    place = (x % 2) * 8 + z * 2 + c
                    target = ((place // nx * nx + place % nx) * nz + y) * 2 + x // 2
                    pairs.append((((y * nx + x) * nz + z) * 2 + c, target))
    return pairs


def in_hbm(*arrays):
    return tuple(pltpu.with_memory_space_constraint(array, pltpu.HBM) for array in arrays)


def after(value, *others):
    return lax.optimization_barrier((value, *others))[0]


def on_device(
    stream,
    projections,
    key_cache,
    value_cache,
    cache_range,
    norm_gain,
    out_weight,
    up_weight,
    down_weight,
):
    width = stream.shape[1]
    half = width // 2
    y, x, z, c = (lax.axis_index(name) for name in "yxzc")
    ny, nx, nz = (lax.axis_size(name) for name in "yxz")
    request = y * nx + x
    unit_rows = up_weight.shape[0]

    place = jnp.stack([c, z, request]).astype(jnp.int32)
    head_rows = lax.ppermute(out_weight, ("y", "x", "z", "c"), head_owners(ny, nx, nz))
    cached = in_hbm(key_cache, value_cache)
    own_query, new_out = pick_new(place, projections)
    new_in = swap_cores(new_out)
    cache_out = pick_cache(after(place, new_out), *cached)
    head_rows = after(head_rows, cache_out)
    weights = lax.all_gather(
        jnp.concatenate([up_weight, down_weight, head_rows], 0), ("y", "x"), axis=0
    )
    (query,) = in_hbm(jnp.concatenate([own_query, new_in[:, :half]], 0))
    queries = [lax.ppermute(query, "z", ring(k, nz)) for k in (2, 1, 3)]
    cache_in = swap_cores(after(cache_out, query))
    context = (*cached, *in_hbm(projections), cache_in, new_in)
    norm_gain, place_late = after((norm_gain, place), *queries, cache_in)
    normed = layer_norm(stream, norm_gain)
    place_late = after(place_late, normed)
    partial, *sent = attend((0, 2, 1, 3), place_late, cache_range, [query, *queries], *context)
    inputs = {k: lax.ppermute(normed, "z", ring(k, nz)) for k in (2, 1, 3)}
    inputs = [normed] + [inputs[k] for k in range(1, nz)]
    sent, inputs = lax.optimization_barrier((sent, inputs))
    partials = [partial] + [
        lax.ppermute(made, "z", ring(-k, nz)) for k, made in zip((2, 1, 3), sent)
    ]
    (own_in,) = in_hbm(jnp.concatenate(inputs, 0))
    (other_in,) = in_hbm(swap_cores(own_in))
    own_hidden, other_hidden = hidden_units(own_in, other_in, *in_hbm(weights), unit_rows)
    heads = merge(after(place, own_hidden), partials)
    attention = {k: lax.ppermute(heads[k], "z", ring(k, nz)) for k in (2, 1, 3)}
    attention = [heads[0]] + [attention[k] for k in range(1, nz)]

    other_hidden, own_hidden = after((other_hidden, own_hidden), heads)
    own_part, other_part = down_units(own_hidden, other_hidden, weights, unit_rows)
    attention = after(tuple(attention), other_part, own_part)
    given = finish(other_part, attention, 1, weights, unit_rows, BF16)
    taken = [swap_cores(part) for part in given]
    kept = finish(after(own_part, *given), attention, 0, weights, unit_rows, F32)
    summed = stream.astype(F32) + kept[0] + taken[0].astype(F32)
    for k in (2, 1, 3):
        both = (kept[k] + taken[k].astype(F32)).astype(BF16)
        summed = summed + lax.ppermute(both, "z", ring(-k, nz)).astype(F32)
    return summed.astype(BF16)


def solution(mesh):
    names = ("y", "x", "z", "c")
    requests, others = mesh.devices.shape
    grid = Mesh(mesh.devices.reshape(requests, others // 8, 4, 2), names)
    rows = P(names, None)
    return jax.shard_map(
        on_device,
        mesh=grid,
        in_specs=(rows, rows, rows, rows, P(), P(), rows, rows, rows),
        out_specs=rows,
        check_vma=False,
    )
```

```python
import functools
import math

import jax
import jax.numpy as jnp
from jax import lax
from jax.experimental import pallas as pl
from jax.experimental.pallas import tpu as pltpu
from jax.sharding import Mesh, PartitionSpec as P

HD = 256
NORM_EPS = 1e-05
NEG = -(2.0**100)
LOG2E = 1.4426950408889634
SCORE = LOG2E / math.sqrt(HD)
MIB = 1 << 20
F32 = jnp.float32
BF16 = jnp.bfloat16


def ring(step, count):
    return [(i, (i + step) % count) for i in range(count)]


def swap_cores(value):
    return lax.ppermute(value, "c", [(0, 1), (1, 0)])


def params(mib):
    return pltpu.CompilerParams(vmem_limit_bytes=mib * MIB)


def dot(a, b, dims):
    return lax.dot_general(a, b, (dims, ((), ())), preferred_element_type=F32)


def pick_new(place, projections):
    rows, width = projections.shape
    heads = width // (2 * HD)

    def body(place_ref, source, own, other):
        c = place_ref[0]
        for j in range(heads):
            other[:, j * HD : (j + 1) * HD] = source[:, pl.ds((2 * j + 1 - c) * HD, HD)]
        for j in range(heads // 3):
            own[:, j * HD : (j + 1) * HD] = source[:, pl.ds((2 * j + c) * HD, HD)]

    return pl.pallas_call(
        body,
        grid_spec=pltpu.PrefetchScalarGridSpec(
            num_scalar_prefetch=1,
            grid=(1,),
            in_specs=[pl.BlockSpec((rows, width), lambda i, s: (0, 0))],
            out_specs=[
                pl.BlockSpec((rows, width // 6), lambda i, s: (0, 0)),
                pl.BlockSpec((rows, width // 2), lambda i, s: (0, 0)),
            ],
        ),
        out_shape=[
            jax.ShapeDtypeStruct((rows, width // 6), BF16),
            jax.ShapeDtypeStruct((rows, width // 2), BF16),
        ],
        compiler_params=params(16),
        name="pick_new",
    )(place, projections)


def pick_cache(place, keys, values):
    rows, width = keys.shape
    heads = width // (2 * HD)

    def body(place_ref, key_ref, value_ref, other, held, arrived, left):
        c = place_ref[0]
        copies = []
        for i, source in enumerate((key_ref, value_ref)):
            for j in range(heads):
                start = pl.multiple_of((2 * j + 1 - c) * HD, HD)
                columns = pl.ds(j * HD, HD)
                slot = held.at[i, :, columns]
                copies.append(
                    (
                        pltpu.make_async_copy(
                            source.at[:, pl.ds(start, HD)], slot, arrived.at[i * heads + j]
                        ),
                        pltpu.make_async_copy(
                            slot, other.at[i, :, columns], left.at[i * heads + j]
                        ),
                    )
                )
        for come, _ in copies:
            come.start()
        for come, leave in copies:
            come.wait()
            leave.start()
        for _, leave in copies:
            leave.wait()

    whole = pl.BlockSpec(memory_space=pl.ANY)
    return pl.pallas_call(
        body,
        grid_spec=pltpu.PrefetchScalarGridSpec(
            num_scalar_prefetch=1,
            grid=(1,),
            in_specs=[whole, whole],
            out_specs=pl.BlockSpec(memory_space=pltpu.HBM),
            scratch_shapes=[
                pltpu.VMEM((2, rows, width // 2), BF16),
                pltpu.SemaphoreType.DMA((2 * heads,)),
                pltpu.SemaphoreType.DMA((2 * heads,)),
            ],
        ),
        out_shape=pltpu.HBM((2, rows, width // 2), BF16),
        compiler_params=params(16),
        name="pick_cache",
    )(place, keys, values)


def norm_kernel(stream, gain, out):
    values = stream[...].astype(F32)
    width = values.shape[1]
    centred = values - jnp.sum(values, axis=-1, keepdims=True) * (1.0 / width)
    spread = jnp.sum(centred * centred, axis=-1, keepdims=True) * (1.0 / width)
    out[...] = (centred * lax.rsqrt(spread + NORM_EPS) * gain[...]).astype(BF16)


def layer_norm(stream, gain):
    return pl.pallas_call(
        norm_kernel,
        out_shape=jax.ShapeDtypeStruct(stream.shape, BF16),
        compiler_params=params(16),
        name="layer_norm",
    )(stream, gain.reshape(1, -1))


def attend_kernel(steps, place, ranges, *refs):
    blocks = len(steps)
    queries, refs = refs[:blocks], refs[blocks:]
    k0, k1, v0, v1, nk0, nk1, nv0, nv1 = refs[:8]
    outs, stats = refs[8 : 8 + blocks], refs[8 + blocks]
    j = pl.program_id(0)
    c, z, request = place[0], place[1], place[2]
    first, end = ranges[request, 0], ranges[request, 1]
    rows = queries[0].shape[0]
    half = rows // 2
    cache_rows = k0.shape[0]
    lane = lax.broadcasted_iota(jnp.int32, stats.shape[1:], 1)

    def bias(member):
        position = member * cache_rows + lax.broadcasted_iota(jnp.int32, (1, cache_rows), 1)
        return jnp.where((position >= first) & (position < end), 0.0, NEG).astype(F32)

    def order(shape, axis):
        place_in = lax.broadcasted_iota(jnp.int32, shape, axis)
        return jnp.where(place_in < half, place_in + c * half, place_in - c * half)

    bias_own, bias_other = bias(2 * z + c), bias(2 * z + 1 - c)
    new_keys = jnp.concatenate([nk0[...], nk1[...]], 0)
    new_values = jnp.concatenate([nv0[...], nv1[...]], 0)
    for i, (step, out) in enumerate(zip(steps, outs)):
        zq = lax.rem(z - step + 4, 4)
        query = queries[i][...]
        score_own = dot(query, k0[...], ((1,), (1,))) + bias_own
        score_other = dot(query, k1[...], ((1,), (1,))) + bias_other
        visible = z * rows + order((1, rows), 1) <= zq * rows + order((rows, 1), 0)
        score_new = jnp.where(visible, dot(query, new_keys, ((1,), (1,))), NEG)
        top = jnp.maximum(
            jnp.maximum(
                jnp.max(score_own, axis=-1, keepdims=True),
                jnp.max(score_other, axis=-1, keepdims=True),
            ),
            jnp.max(score_new, axis=-1, keepdims=True),
        )
        shift = top.astype(BF16).astype(F32)

        def weigh(score, values):
            weight = jnp.exp2((score - shift) * SCORE)
            return (
                jnp.sum(weight, axis=-1, keepdims=True),
                dot(weight.astype(BF16), values, ((1,), (0,))),
            )

        parts = [
            weigh(score_own, v0[...]),
            weigh(score_other, v1[...]),
            weigh(score_new, new_values),
        ]
        total = parts[0][0] + parts[1][0] + parts[2][0]
        out[:, pl.ds(pl.multiple_of(j * HD, HD), HD)] = (
            parts[0][1] + parts[1][1] + parts[2][1]
        ).astype(BF16)
        high = total.astype(BF16).astype(F32)
        kept = jnp.where(j == 0, 0.0, stats[i])
        kept = jnp.where(lane == 3 * j, shift, kept)
        kept = jnp.where(lane == 3 * j + 1, high, kept)
        kept = jnp.where(lane == 3 * j + 2, total - high, kept)
        stats[i] = kept
        out[:, out.shape[1] - 128 :] = kept.astype(BF16)


def attend(steps, place, ranges, queries, keys, values, projections, cache_in, new_in):
    rows, width = queries[0].shape
    blocks = len(steps)
    heads = width // HD
    cache_rows = keys.shape[0]
    new_rows = projections.shape[0]

    def columns(count, index):
        return pl.BlockSpec((count, HD), index)

    def received(i):
        return pl.BlockSpec((None, cache_rows, HD), lambda j, s, r: (i, 0, j))

    return pl.pallas_call(
        functools.partial(attend_kernel, steps),
        grid_spec=pltpu.PrefetchScalarGridSpec(
            num_scalar_prefetch=2,
            grid=(heads,),
            in_specs=[columns(rows, lambda j, s, r: (0, j))] * blocks
            + [
                columns(cache_rows, lambda j, s, r: (0, 2 * j + s[0])),
                received(0),
                columns(cache_rows, lambda j, s, r: (0, 2 * j + s[0])),
                received(1),
                columns(new_rows, lambda j, s, r: (0, 2 * heads + 2 * j + s[0])),
                columns(new_rows, lambda j, s, r: (0, heads + j)),
                columns(new_rows, lambda j, s, r: (0, 4 * heads + 2 * j + s[0])),
                columns(new_rows, lambda j, s, r: (0, 2 * heads + j)),
            ],
            out_specs=[pl.BlockSpec((rows, width + 128), lambda j, s, r: (0, 0))] * blocks,
            scratch_shapes=[pltpu.VMEM((blocks, rows, 128), F32)],
        ),
        out_shape=[jax.ShapeDtypeStruct((rows, width + 128), BF16)] * blocks,
        compiler_params=params(40),
        cost_estimate=pl.CostEstimate(
            flops=4 * blocks * rows * (2 * cache_rows + rows) * width,
            transcendentals=blocks * rows * (2 * cache_rows + rows) * heads,
            bytes_accessed=8 * cache_rows * width + 8 * blocks * rows * width,
        ),
        name="attend",
    )(
        place,
        ranges,
        *queries,
        keys,
        cache_in,
        values,
        cache_in,
        projections,
        new_in,
        projections,
        new_in,
    )


def merge_kernel(place, a, b, c, d, out):
    z = place[1]
    count = out.shape[0]
    parts = (a, b, c, d)
    base = a.shape[1] - 128
    stats = [part[:, base:].astype(F32) for part in parts]
    for j in range(count):
        shifts = [s[:, 3 * j : 3 * j + 1] for s in stats]
        totals = [s[:, 3 * j + 1 : 3 * j + 2] + s[:, 3 * j + 2 : 3 * j + 3] for s in stats]
        top = jnp.maximum(
            jnp.maximum(shifts[0], shifts[1]), jnp.maximum(shifts[2], shifts[3])
        )
        factors = [jnp.exp2((s - top) * SCORE) for s in shifts]
        total = sum(f * t for f, t in zip(factors, totals))
        summed = sum(
            f * part[:, j * HD : (j + 1) * HD].astype(F32) for f, part in zip(factors, parts)
        )
        out[lax.rem(j - z + count, count)] = (summed / total).astype(BF16)


def merge(place, parts):
    rows, width = parts[0].shape
    count = (width - 128) // HD
    whole = pl.BlockSpec((rows, width), lambda i, s: (0, 0))
    return pl.pallas_call(
        merge_kernel,
        grid_spec=pltpu.PrefetchScalarGridSpec(
            num_scalar_prefetch=1,
            grid=(1,),
            in_specs=[whole] * 4,
            out_specs=pl.BlockSpec((count, rows, HD), lambda i, s: (0, 0, 0)),
        ),
        out_shape=jax.ShapeDtypeStruct((count, rows, HD), BF16),
        compiler_params=params(12),
        name="merge",
    )(place, *parts)


def hidden_kernel(own_in, other_in, up_ref, own, other):
    shards, rows, width = up_ref.shape
    up = up_ref[...].reshape(shards * rows, width)
    for inputs, out in ((own_in, own), (other_in, other)):
        gates = dot(inputs[...], up, ((1,), (1,)))
        out[...] = (0.5 * gates * (1.0 + lax.erf(gates * math.sqrt(0.5)))).astype(BF16)


def hidden_units(own_in, other_in, weights, unit_rows):
    rows, width = own_in.shape
    shards = weights.shape[0]
    chunk = 4
    count = chunk * unit_rows
    whole = pl.BlockSpec((rows, width), lambda i: (0, 0))
    part = pl.BlockSpec((rows, count), lambda i: (0, i))
    return pl.pallas_call(
        hidden_kernel,
        grid=(shards // chunk,),
        in_specs=[
            whole,
            whole,
            pl.BlockSpec((chunk, unit_rows, width), lambda i: (i, 0, 0)),
        ],
        out_specs=[part, part],
        out_shape=[jax.ShapeDtypeStruct((rows, shards * unit_rows), BF16)] * 2,
        compiler_params=params(20),
        cost_estimate=pl.CostEstimate(
            flops=4 * rows * shards * unit_rows * width,
            transcendentals=0,
            bytes_accessed=2 * shards * unit_rows * width + 4 * rows * width,
        ),
        name="hidden_units",
    )(own_in, other_in, weights)


def down_kernel(own_hidden, other_hidden, down_ref, own, other):
    shards, rows, columns = down_ref.shape
    down = down_ref[...].reshape(shards * rows, columns)
    other[...] = dot(other_hidden[...], down, ((1,), (0,)))
    own[...] = dot(own_hidden[...], down, ((1,), (0,)))


def down_units(own_hidden, other_hidden, weights, unit_rows):
    rows, units = own_hidden.shape
    shards, _, width = weights.shape
    columns = 512
    whole = pl.BlockSpec((rows, units), lambda i: (0, 0))
    part = pl.BlockSpec((rows, columns), lambda i: (0, i))
    return pl.pallas_call(
        down_kernel,
        grid=(width // columns,),
        in_specs=[
            whole,
            whole,
            pl.BlockSpec((shards, unit_rows, columns), lambda i: (0, 1, i)),
        ],
        out_specs=[part, part],
        out_shape=[jax.ShapeDtypeStruct((rows, width), F32)] * 2,
        compiler_params=params(20),
        cost_estimate=pl.CostEstimate(
            flops=4 * rows * units * width,
            transcendentals=0,
            bytes_accessed=2 * units * width + 4 * rows * units + 8 * rows * width,
        ),
        name="down_units",
    )(own_hidden, other_hidden, weights)


def finish_kernel(partial, a0, a1, a2, a3, out_ref, *outs):
    shards, rows, columns = out_ref.shape
    heads = jnp.concatenate([a0[...], a1[...], a2[...], a3[...]], 0)
    out_rows = out_ref[...].reshape(shards * rows, columns)
    made = partial[...] + dot(heads, out_rows, ((1,), (0,)))
    count = made.shape[0] // len(outs)
    for i, out in enumerate(outs):
        out[...] = made[i * count : (i + 1) * count].astype(out.dtype)


def finish(partial, heads, side, weights, unit_rows, dtype):
    rows, width = partial.shape
    shards, shard_rows, _ = weights.shape
    out_rows = shard_rows - 2 * unit_rows
    count = rows // len(heads)
    columns = 512
    return pl.pallas_call(
        finish_kernel,
        grid=(width // columns,),
        in_specs=[pl.BlockSpec((rows, columns), lambda i: (0, i))]
        + [pl.BlockSpec((count, HD), lambda i: (side, 0))] * len(heads)
        + [
            pl.BlockSpec(
                (shards, out_rows, columns), lambda i: (0, 2 * unit_rows // out_rows, i)
            ),
        ],
        out_specs=[pl.BlockSpec((count, columns), lambda i: (0, i))] * len(heads),
        out_shape=[jax.ShapeDtypeStruct((count, width), dtype)] * len(heads),
        compiler_params=params(16),
        cost_estimate=pl.CostEstimate(
            flops=2 * rows * HD * width,
            transcendentals=0,
            bytes_accessed=2 * HD * width + 8 * rows * width,
        ),
        name="finish",
    )(partial, *heads, weights)


def head_owners(ny, nx, nz):
    pairs = []
    for y in range(ny):
        for x in range(nx):
            for z in range(nz):
                for c in range(2):
                    place = (x % 2) * 8 + z * 2 + c
                    target = ((place // nx * nx + place % nx) * nz + y) * 2 + x // 2
                    pairs.append((((y * nx + x) * nz + z) * 2 + c, target))
    return pairs


def in_hbm(*arrays):
    return tuple(pltpu.with_memory_space_constraint(array, pltpu.HBM) for array in arrays)


def after(value, *others):
    return lax.optimization_barrier((value, *others))[0]


def on_device(
    stream,
    projections,
    key_cache,
    value_cache,
    cache_range,
    norm_gain,
    out_weight,
    up_weight,
    down_weight,
):
    width = stream.shape[1]
    half = width // 2
    y, x, z, c = (lax.axis_index(name) for name in "yxzc")
    ny, nx, nz = (lax.axis_size(name) for name in "yxz")
    request = y * nx + x
    unit_rows = up_weight.shape[0]

    place = jnp.stack([c, z, request]).astype(jnp.int32)
    head_rows = lax.ppermute(out_weight, ("y", "x", "z", "c"), head_owners(ny, nx, nz))
    cached = in_hbm(key_cache, value_cache)
    own_query, new_out = pick_new(place, projections)
    new_in = swap_cores(new_out)
    cache_out = pick_cache(after(place, new_out), *cached)
    head_rows = after(head_rows, cache_out)
    weights = lax.all_gather(
        jnp.concatenate([up_weight, down_weight, head_rows], 0), ("y", "x"), axis=0
    )
    query = jnp.concatenate([own_query, new_in[:, :half]], 0)
    queries = [lax.ppermute(query, "z", ring(k, nz)) for k in (2, 1, 3)]
    cache_in = swap_cores(after(cache_out, query))
    context = (*cached, *in_hbm(projections), cache_in, new_in)
    norm_gain, place_late = after((norm_gain, place), *queries, cache_in)
    normed = layer_norm(stream, norm_gain)
    place_late = after(place_late, normed)
    partial, *sent = attend((0, 2, 1, 3), place_late, cache_range, [query, *queries], *context)
    inputs = [normed] + [lax.ppermute(normed, "z", ring(k, nz)) for k in range(1, nz)]
    sent, inputs = lax.optimization_barrier((sent, inputs))
    partials = [partial] + [
        lax.ppermute(made, "z", ring(-k, nz)) for k, made in zip((2, 1, 3), sent)
    ]
    (own_in,) = in_hbm(jnp.concatenate(inputs, 0))
    (other_in,) = in_hbm(swap_cores(own_in))
    own_hidden, other_hidden = hidden_units(own_in, other_in, *in_hbm(weights), unit_rows)
    heads = merge(after(place, own_hidden), partials)
    attention = [heads[0]] + [lax.ppermute(heads[k], "z", ring(k, nz)) for k in range(1, nz)]

    other_hidden, own_hidden = after((other_hidden, own_hidden), heads)
    own_part, other_part = down_units(own_hidden, other_hidden, weights, unit_rows)
    attention = after(tuple(attention), other_part, own_part)
    given = finish(other_part, attention, 1, weights, unit_rows, BF16)
    taken = [swap_cores(part) for part in given]
    kept = finish(after(own_part, *given), attention, 0, weights, unit_rows, F32)
    summed = stream.astype(F32) + kept[0] + taken[0].astype(F32)
    for k in (2, 1, 3):
        both = (kept[k] + taken[k].astype(F32)).astype(BF16)
        summed = summed + lax.ppermute(both, "z", ring(-k, nz)).astype(F32)
    return summed.astype(BF16)


def solution(mesh):
    names = ("y", "x", "z", "c")
    requests, others = mesh.devices.shape
    grid = Mesh(mesh.devices.reshape(requests, others // 8, 4, 2), names)
    rows = P(names, None)
    return jax.shard_map(
        on_device,
        mesh=grid,
        in_specs=(rows, rows, rows, rows, P(), P(), rows, rows, rows),
        out_specs=rows,
        check_vma=False,
    )
```

```python
import functools
import math

import jax
import jax.numpy as jnp
from jax import lax
from jax.experimental import pallas as pl
from jax.experimental.pallas import tpu as pltpu
from jax.sharding import Mesh, PartitionSpec as P

HD = 256
NORM_EPS = 1e-05
NEG = -(2.0**100)
LOG2E = 1.4426950408889634
SCORE = LOG2E / math.sqrt(HD)
MIB = 1 << 20
F32 = jnp.float32
BF16 = jnp.bfloat16


def ring(step, count):
    return [(i, (i + step) % count) for i in range(count)]


def swap_cores(value):
    return lax.ppermute(value, "c", [(0, 1), (1, 0)])


def params(mib):
    return pltpu.CompilerParams(vmem_limit_bytes=mib * MIB)


def dot(a, b, dims):
    return lax.dot_general(a, b, (dims, ((), ())), preferred_element_type=F32)


def pick_new(place, projections):
    rows, width = projections.shape
    heads = width // (2 * HD)

    def body(place_ref, source, own, other):
        c = place_ref[0]
        for j in range(heads):
            other[:, j * HD : (j + 1) * HD] = source[:, pl.ds((2 * j + 1 - c) * HD, HD)]
        for j in range(heads // 3):
            own[:, j * HD : (j + 1) * HD] = source[:, pl.ds((2 * j + c) * HD, HD)]

    return pl.pallas_call(
        body,
        grid_spec=pltpu.PrefetchScalarGridSpec(
            num_scalar_prefetch=1,
            grid=(1,),
            in_specs=[pl.BlockSpec((rows, width), lambda i, s: (0, 0))],
            out_specs=[
                pl.BlockSpec((rows, width // 6), lambda i, s: (0, 0)),
                pl.BlockSpec((rows, width // 2), lambda i, s: (0, 0)),
            ],
        ),
        out_shape=[
            jax.ShapeDtypeStruct((rows, width // 6), BF16),
            jax.ShapeDtypeStruct((rows, width // 2), BF16),
        ],
        compiler_params=params(16),
        name="pick_new",
    )(place, projections)


def pick_cache(place, keys, values):
    rows, width = keys.shape
    heads = width // (2 * HD)

    def body(place_ref, key_ref, value_ref, other, held, arrived, left):
        c = place_ref[0]
        copies = []
        for i, source in enumerate((key_ref, value_ref)):
            for j in range(heads):
                start = pl.multiple_of((2 * j + 1 - c) * HD, HD)
                columns = pl.ds(j * HD, HD)
                slot = held.at[i, :, columns]
                copies.append(
                    (
                        pltpu.make_async_copy(
                            source.at[:, pl.ds(start, HD)], slot, arrived.at[i * heads + j]
                        ),
                        pltpu.make_async_copy(
                            slot, other.at[i, :, columns], left.at[i * heads + j]
                        ),
                    )
                )
        for come, _ in copies:
            come.start()
        for come, leave in copies:
            come.wait()
            leave.start()
        for _, leave in copies:
            leave.wait()

    whole = pl.BlockSpec(memory_space=pl.ANY)
    return pl.pallas_call(
        body,
        grid_spec=pltpu.PrefetchScalarGridSpec(
            num_scalar_prefetch=1,
            grid=(1,),
            in_specs=[whole, whole],
            out_specs=pl.BlockSpec(memory_space=pltpu.HBM),
            scratch_shapes=[
                pltpu.VMEM((2, rows, width // 2), BF16),
                pltpu.SemaphoreType.DMA((2 * heads,)),
                pltpu.SemaphoreType.DMA((2 * heads,)),
            ],
        ),
        out_shape=pltpu.HBM((2, rows, width // 2), BF16),
        compiler_params=params(16),
        name="pick_cache",
    )(place, keys, values)


def norm_kernel(stream, gain, out):
    values = stream[...].astype(F32)
    width = values.shape[1]
    centred = values - jnp.sum(values, axis=-1, keepdims=True) * (1.0 / width)
    spread = jnp.sum(centred * centred, axis=-1, keepdims=True) * (1.0 / width)
    out[...] = (centred * lax.rsqrt(spread + NORM_EPS) * gain[...]).astype(BF16)


def layer_norm(stream, gain):
    return pl.pallas_call(
        norm_kernel,
        out_shape=jax.ShapeDtypeStruct(stream.shape, BF16),
        compiler_params=params(16),
        name="layer_norm",
    )(stream, gain.reshape(1, -1))


def attend_kernel(steps, place, ranges, *refs):
    blocks = len(steps)
    queries, refs = refs[:blocks], refs[blocks:]
    k0, k1, v0, v1, nk0, nk1, nv0, nv1 = refs[:8]
    outs, stats = refs[8 : 8 + blocks], refs[8 + blocks]
    j = pl.program_id(0)
    c, z, request = place[0], place[1], place[2]
    first, end = ranges[request, 0], ranges[request, 1]
    rows = queries[0].shape[0]
    half = rows // 2
    cache_rows = k0.shape[0]
    lane = lax.broadcasted_iota(jnp.int32, stats.shape[1:], 1)

    def bias(member):
        position = member * cache_rows + lax.broadcasted_iota(jnp.int32, (1, cache_rows), 1)
        return jnp.where((position >= first) & (position < end), 0.0, NEG).astype(F32)

    def order(shape, axis):
        place_in = lax.broadcasted_iota(jnp.int32, shape, axis)
        return jnp.where(place_in < half, place_in + c * half, place_in - c * half)

    bias_own, bias_other = bias(2 * z + c), bias(2 * z + 1 - c)
    new_keys = jnp.concatenate([nk0[...], nk1[...]], 0)
    new_values = jnp.concatenate([nv0[...], nv1[...]], 0)
    for i, (step, out) in enumerate(zip(steps, outs)):
        zq = lax.rem(z - step + 4, 4)
        query = queries[i][...]
        score_own = dot(query, k0[...], ((1,), (1,))) + bias_own
        score_other = dot(query, k1[...], ((1,), (1,))) + bias_other
        visible = z * rows + order((1, rows), 1) <= zq * rows + order((rows, 1), 0)
        score_new = jnp.where(visible, dot(query, new_keys, ((1,), (1,))), NEG)
        top = jnp.maximum(
            jnp.maximum(
                jnp.max(score_own, axis=-1, keepdims=True),
                jnp.max(score_other, axis=-1, keepdims=True),
            ),
            jnp.max(score_new, axis=-1, keepdims=True),
        )
        shift = top.astype(BF16).astype(F32)

        def weigh(score, values):
            weight = jnp.exp2((score - shift) * SCORE)
            return (
                jnp.sum(weight, axis=-1, keepdims=True),
                dot(weight.astype(BF16), values, ((1,), (0,))),
            )

        parts = [
            weigh(score_own, v0[...]),
            weigh(score_other, v1[...]),
            weigh(score_new, new_values),
        ]
        total = parts[0][0] + parts[1][0] + parts[2][0]
        out[:, pl.ds(pl.multiple_of(j * HD, HD), HD)] = (
            parts[0][1] + parts[1][1] + parts[2][1]
        ).astype(BF16)
        high = total.astype(BF16).astype(F32)
        kept = jnp.where(j == 0, 0.0, stats[i])
        kept = jnp.where(lane == 3 * j, shift, kept)
        kept = jnp.where(lane == 3 * j + 1, high, kept)
        kept = jnp.where(lane == 3 * j + 2, total - high, kept)
        stats[i] = kept
        out[:, out.shape[1] - 128 :] = kept.astype(BF16)


def attend(steps, place, ranges, queries, keys, values, projections, cache_in, new_in):
    rows, width = queries[0].shape
    blocks = len(steps)
    heads = width // HD
    cache_rows = keys.shape[0]
    new_rows = projections.shape[0]

    def columns(count, index):
        return pl.BlockSpec((count, HD), index)

    def received(i):
        return pl.BlockSpec((None, cache_rows, HD), lambda j, s, r: (i, 0, j))

    return pl.pallas_call(
        functools.partial(attend_kernel, steps),
        grid_spec=pltpu.PrefetchScalarGridSpec(
            num_scalar_prefetch=2,
            grid=(heads,),
            in_specs=[columns(rows, lambda j, s, r: (0, j))] * blocks
            + [
                columns(cache_rows, lambda j, s, r: (0, 2 * j + s[0])),
                received(0),
                columns(cache_rows, lambda j, s, r: (0, 2 * j + s[0])),
                received(1),
                columns(new_rows, lambda j, s, r: (0, 2 * heads + 2 * j + s[0])),
                columns(new_rows, lambda j, s, r: (0, heads + j)),
                columns(new_rows, lambda j, s, r: (0, 4 * heads + 2 * j + s[0])),
                columns(new_rows, lambda j, s, r: (0, 2 * heads + j)),
            ],
            out_specs=[pl.BlockSpec((rows, width + 128), lambda j, s, r: (0, 0))] * blocks,
            scratch_shapes=[pltpu.VMEM((blocks, rows, 128), F32)],
        ),
        out_shape=[jax.ShapeDtypeStruct((rows, width + 128), BF16)] * blocks,
        compiler_params=params(40),
        cost_estimate=pl.CostEstimate(
            flops=4 * blocks * rows * (2 * cache_rows + rows) * width,
            transcendentals=blocks * rows * (2 * cache_rows + rows) * heads,
            bytes_accessed=8 * cache_rows * width + 8 * blocks * rows * width,
        ),
        name="attend",
    )(
        place,
        ranges,
        *queries,
        keys,
        cache_in,
        values,
        cache_in,
        projections,
        new_in,
        projections,
        new_in,
    )


def merge_kernel(place, a, b, c, d, out):
    z = place[1]
    count = out.shape[0]
    parts = (a, b, c, d)
    base = a.shape[1] - 128
    stats = [part[:, base:].astype(F32) for part in parts]
    for j in range(count):
        shifts = [s[:, 3 * j : 3 * j + 1] for s in stats]
        totals = [s[:, 3 * j + 1 : 3 * j + 2] + s[:, 3 * j + 2 : 3 * j + 3] for s in stats]
        top = jnp.maximum(
            jnp.maximum(shifts[0], shifts[1]), jnp.maximum(shifts[2], shifts[3])
        )
        factors = [jnp.exp2((s - top) * SCORE) for s in shifts]
        total = sum(f * t for f, t in zip(factors, totals))
        summed = sum(
            f * part[:, j * HD : (j + 1) * HD].astype(F32) for f, part in zip(factors, parts)
        )
        out[lax.rem(j - z + count, count)] = (summed / total).astype(BF16)


def merge(place, parts):
    rows, width = parts[0].shape
    count = (width - 128) // HD
    whole = pl.BlockSpec((rows, width), lambda i, s: (0, 0))
    return pl.pallas_call(
        merge_kernel,
        grid_spec=pltpu.PrefetchScalarGridSpec(
            num_scalar_prefetch=1,
            grid=(1,),
            in_specs=[whole] * 4,
            out_specs=pl.BlockSpec((count, rows, HD), lambda i, s: (0, 0, 0)),
        ),
        out_shape=jax.ShapeDtypeStruct((count, rows, HD), BF16),
        compiler_params=params(12),
        name="merge",
    )(place, *parts)


def hidden_kernel(own_in, other_in, up_ref, own, other):
    shards, rows, width = up_ref.shape
    up = up_ref[...].reshape(shards * rows, width)
    for inputs, out in ((own_in, own), (other_in, other)):
        gates = dot(inputs[...], up, ((1,), (1,)))
        out[...] = (0.5 * gates * (1.0 + lax.erf(gates * math.sqrt(0.5)))).astype(BF16)


def hidden_units(own_in, other_in, weights, unit_rows):
    rows, width = own_in.shape
    shards = weights.shape[0]
    chunk = 4
    count = chunk * unit_rows
    whole = pl.BlockSpec((rows, width), lambda i: (0, 0))
    part = pl.BlockSpec((rows, count), lambda i: (0, i))
    return pl.pallas_call(
        hidden_kernel,
        grid=(shards // chunk,),
        in_specs=[
            whole,
            whole,
            pl.BlockSpec((chunk, unit_rows, width), lambda i: (i, 0, 0)),
        ],
        out_specs=[part, part],
        out_shape=[jax.ShapeDtypeStruct((rows, shards * unit_rows), BF16)] * 2,
        compiler_params=params(20),
        cost_estimate=pl.CostEstimate(
            flops=4 * rows * shards * unit_rows * width,
            transcendentals=0,
            bytes_accessed=2 * shards * unit_rows * width + 4 * rows * width,
        ),
        name="hidden_units",
    )(own_in, other_in, weights)


def down_kernel(own_hidden, other_hidden, down_ref, own, other):
    shards, rows, columns = down_ref.shape
    down = down_ref[...].reshape(shards * rows, columns)
    other[...] = dot(other_hidden[...], down, ((1,), (0,)))
    own[...] = dot(own_hidden[...], down, ((1,), (0,)))


def down_units(own_hidden, other_hidden, weights, unit_rows):
    rows, units = own_hidden.shape
    shards, _, width = weights.shape
    columns = 512
    whole = pl.BlockSpec((rows, units), lambda i: (0, 0))
    part = pl.BlockSpec((rows, columns), lambda i: (0, i))
    return pl.pallas_call(
        down_kernel,
        grid=(width // columns,),
        in_specs=[
            whole,
            whole,
            pl.BlockSpec((shards, unit_rows, columns), lambda i: (0, 1, i)),
        ],
        out_specs=[part, part],
        out_shape=[jax.ShapeDtypeStruct((rows, width), F32)] * 2,
        compiler_params=params(20),
        cost_estimate=pl.CostEstimate(
            flops=4 * rows * units * width,
            transcendentals=0,
            bytes_accessed=2 * units * width + 4 * rows * units + 8 * rows * width,
        ),
        name="down_units",
    )(own_hidden, other_hidden, weights)


def finish_kernel(partial, a0, a1, a2, a3, out_ref, *outs):
    shards, rows, columns = out_ref.shape
    heads = jnp.concatenate([a0[...], a1[...], a2[...], a3[...]], 0)
    out_rows = out_ref[...].reshape(shards * rows, columns)
    made = partial[...] + dot(heads, out_rows, ((1,), (0,)))
    count = made.shape[0] // len(outs)
    for i, out in enumerate(outs):
        out[...] = made[i * count : (i + 1) * count].astype(out.dtype)


def finish(partial, heads, side, weights, unit_rows, dtype):
    rows, width = partial.shape
    shards, shard_rows, _ = weights.shape
    out_rows = shard_rows - 2 * unit_rows
    count = rows // len(heads)
    columns = 1024
    return pl.pallas_call(
        finish_kernel,
        grid=(width // columns,),
        in_specs=[pl.BlockSpec((rows, columns), lambda i: (0, i))]
        + [pl.BlockSpec((count, HD), lambda i: (side, 0))] * len(heads)
        + [
            pl.BlockSpec(
                (shards, out_rows, columns), lambda i: (0, 2 * unit_rows // out_rows, i)
            ),
        ],
        out_specs=[pl.BlockSpec((count, columns), lambda i: (0, i))] * len(heads),
        out_shape=[jax.ShapeDtypeStruct((count, width), dtype)] * len(heads),
        compiler_params=params(16),
        cost_estimate=pl.CostEstimate(
            flops=2 * rows * HD * width,
            transcendentals=0,
            bytes_accessed=2 * HD * width + 8 * rows * width,
        ),
        name="finish",
    )(partial, *heads, weights)


def head_owners(ny, nx, nz):
    pairs = []
    for y in range(ny):
        for x in range(nx):
            for z in range(nz):
                for c in range(2):
                    place = (x % 2) * 8 + z * 2 + c
                    target = ((place // nx * nx + place % nx) * nz + y) * 2 + x // 2
                    pairs.append((((y * nx + x) * nz + z) * 2 + c, target))
    return pairs


def in_hbm(*arrays):
    return tuple(pltpu.with_memory_space_constraint(array, pltpu.HBM) for array in arrays)


def after(value, *others):
    return lax.optimization_barrier((value, *others))[0]


def on_device(
    stream,
    projections,
    key_cache,
    value_cache,
    cache_range,
    norm_gain,
    out_weight,
    up_weight,
    down_weight,
):
    width = stream.shape[1]
    half = width // 2
    y, x, z, c = (lax.axis_index(name) for name in "yxzc")
    ny, nx, nz = (lax.axis_size(name) for name in "yxz")
    request = y * nx + x
    unit_rows = up_weight.shape[0]

    place = jnp.stack([c, z, request]).astype(jnp.int32)
    head_rows = lax.ppermute(out_weight, ("y", "x", "z", "c"), head_owners(ny, nx, nz))
    cached = in_hbm(key_cache, value_cache)
    own_query, new_out = pick_new(place, projections)
    new_in = swap_cores(new_out)
    cache_out = pick_cache(after(place, new_out), *cached)
    head_rows = after(head_rows, cache_out)
    weights = lax.all_gather(
        jnp.concatenate([up_weight, down_weight, head_rows], 0), ("y", "x"), axis=0
    )
    (query,) = in_hbm(jnp.concatenate([own_query, new_in[:, :half]], 0))
    queries = [lax.ppermute(query, "z", ring(k, nz)) for k in (2, 1, 3)]
    cache_in = swap_cores(after(cache_out, query))
    context = (*cached, *in_hbm(projections), cache_in, new_in)
    norm_gain, place_late = after((norm_gain, place), *queries, cache_in)
    normed = layer_norm(stream, norm_gain)
    place_late = after(place_late, normed)
    partial, *sent = attend((0, 2, 1, 3), place_late, cache_range, [query, *queries], *context)
    inputs = [normed] + [lax.ppermute(normed, "z", ring(k, nz)) for k in range(1, nz)]
    sent, inputs = lax.optimization_barrier((sent, inputs))
    partials = [partial] + [
        lax.ppermute(made, "z", ring(-k, nz)) for k, made in zip((2, 1, 3), sent)
    ]
    (own_in,) = in_hbm(jnp.concatenate(inputs, 0))
    (other_in,) = in_hbm(swap_cores(own_in))
    own_hidden, other_hidden = hidden_units(own_in, other_in, *in_hbm(weights), unit_rows)
    heads = merge(after(place, own_hidden), partials)
    attention = [heads[0]] + [lax.ppermute(heads[k], "z", ring(k, nz)) for k in range(1, nz)]

    other_hidden, own_hidden = after((other_hidden, own_hidden), heads)
    own_part, other_part = down_units(own_hidden, other_hidden, weights, unit_rows)
    attention = after(tuple(attention), other_part, own_part)
    given = finish(other_part, attention, 1, weights, unit_rows, BF16)
    taken = [swap_cores(part) for part in given]
    kept = finish(after(own_part, *given), attention, 0, weights, unit_rows, F32)
    summed = stream.astype(F32) + kept[0] + taken[0].astype(F32)
    for k in (2, 1, 3):
        both = (kept[k] + taken[k].astype(F32)).astype(BF16)
        summed = summed + lax.ppermute(both, "z", ring(-k, nz)).astype(F32)
    return summed.astype(BF16)


def solution(mesh):
    names = ("y", "x", "z", "c")
    requests, others = mesh.devices.shape
    grid = Mesh(mesh.devices.reshape(requests, others // 8, 4, 2), names)
    rows = P(names, None)
    return jax.shard_map(
        on_device,
        mesh=grid,
        in_specs=(rows, rows, rows, rows, P(), P(), rows, rows, rows),
        out_specs=rows,
        check_vma=False,
    )
```
